32 devices in a mesh: groups: 2 (over y), tmpl: 16 (over z, x, core).
Axes of the slice: x: 2, y: 2, z: 4, core: 2. Of those that a mesh axis runs over, the one named last changes fastest.
Arguments:
- records: bfloat16 [512, 3, 768], P(('groups', 'tmpl')), parts along dimension 0, may hold values from -200 to 200, as said below
- templates: bfloat16 [96, 20, 3, 300], P('tmpl'), may hold values from -6 to 6
- fetch_list: int32 [16, 16, 2], P('tmpl'), may hold values from -1 to 15, as said below
- cluster_slots: int32 [96, 20], P('tmpl'), may hold values from 0 to 31, as said below
- moveouts: int32 [96, 20], P('tmpl'), may hold values from 0 to 213
Outputs:
- stack: float32 [192, 256], P(('groups', 'tmpl')), parts along dimension 0
- network_peak: float32 [512], P('groups'), parts along dimension 0
The draws below stay inside these ranges and needn't reach their ends.
There are 2 independent parts, one for each index of `groups`. The reference program is written for one: setup_inputs(seed, part) draws one part's arguments, and reference() takes and returns one part's arrays. A program takes and returns all parts, laid end to end along the dimension named above; an argument that names none is the same for every part. Nothing has to cross between parts.
Inputs may be any that keep to these rules, and one draw needn't show every extreme that they name: Values are the records' samples; the amplitude of a station component is steady apart from one event burst. fetch_list[g, o, s] is an index among holder o's 16 stations, or -1 for an empty slot; the set entries of one (g, o) pair differ; every group g has all 2 slots set for the holders g to g + 20 // 2 - 1 (modulo 16). cluster_slots[k, j] is a slot o * 2 + s of group k // 6 whose fetch_list entry is set; the 20 entries of a station set differ, and every set slot of a group is named by some station set of that group.
All inputs are finite; a program needn't handle non-finite values.
Results may differ from the reference program's by a relative error of at most 0.0003.
Values may be sent and summed in bfloat16 or wider, within the bound.
A program may use at most 64 MiB of HBM per device.

```python
import math
import jax
import jax.numpy as jnp
from jax import lax

NSTAT = 20
TAPS = 300
OUT = 256
STA_DEV = 16
CAP = 2
CLUST = 6
TPC = 1
REC = 768
MOVE = 214
OWNERS = 16
STATIONS = 256
TEMPLATES = 96


def draw_plan(key):
    seed_key = jax.random.fold_in(key, 4051)
    key_rank, key_count, key_pick, key_shuffle = jax.random.split(seed_key, 4)
    owners = OWNERS
    slot_count = OWNERS * CAP
    group_ids = jnp.arange(owners, dtype=jnp.int32)[:, None, None]
    owner_ids = jnp.arange(owners, dtype=jnp.int32)[None, :, None]
    distance = (owner_ids - group_ids) % owners
    forced = jnp.broadcast_to(distance < NSTAT // CAP, (owners, owners, CAP)).reshape(owners, slot_count)
    column = jnp.arange(slot_count, dtype=jnp.int32)[None, :]
    spread = 2 ** 18
    scores = jax.random.randint(key_rank, (owners, slot_count), 0, spread) * slot_count + column + forced.astype(jnp.int32) * (spread * slot_count)
    ranking = jnp.argsort(-scores, axis=1)
    placing = jnp.argsort(ranking, axis=1)
    lowest = max(NSTAT, slot_count * 2 // 5)
    highest = min(CLUST * NSTAT, slot_count)
    live_count = jax.random.randint(key_count, (owners, 1), lowest, highest + 1)
    filled = placing < live_count
    keyed = jax.random.randint(key_pick, (owners, owners, STA_DEV), 0, spread) * STA_DEV + jnp.arange(STA_DEV, dtype=jnp.int32)
    picked = jnp.argsort(keyed, axis=2)[:, :, :CAP].astype(jnp.int32)
    fetch_ids = jnp.where(filled.reshape(owners, owners, CAP), picked, -1).astype(jnp.int32)
    shuffle = jnp.where(filled, jax.random.randint(key_shuffle, (owners, slot_count), 0, spread) * slot_count + column, spread * slot_count + column)
    listed = jnp.argsort(shuffle, axis=1).astype(jnp.int32)
    position = (jnp.arange(CLUST, dtype=jnp.int32)[:, None] * NSTAT + jnp.arange(NSTAT, dtype=jnp.int32)[None, :]).reshape(1, CLUST * NSTAT) % live_count
    chosen = jnp.take_along_axis(listed, position, axis=1)
    return (fetch_ids, chosen.reshape(owners * CLUST, NSTAT).astype(jnp.int32))


def draw_fetch_list(key, part):
    fetch_ids, chosen = draw_plan(key)
    return fetch_ids


def draw_cluster_slots(key, part):
    fetch_ids, chosen = draw_plan(key)
    return chosen


def draw_records(key, part):
    key_noise, key_scale, key_centre, key_width = jax.random.split(jax.random.fold_in(key, 911), 4)
    shape = (STATIONS, 3, REC)
    noise = jax.random.truncated_normal(key_noise, -5.0, 5.0, shape, jnp.float32)
    amplitude = jnp.exp(jax.random.uniform(key_scale, (STATIONS, 3, 1), jnp.float32, 0.0, math.log(10.0)))
    centre = jax.random.uniform(key_centre, (STATIONS, 1, 1), jnp.float32, 0.0, REC)
    breadth = jax.random.uniform(key_width, (STATIONS, 1, 1), jnp.float32, REC / 32.0, REC / 8.0)
    times = jnp.arange(REC, dtype=jnp.float32)[None, None, :]
    envelope = 1.0 + 3.0 * jnp.exp(-((times - centre) / breadth) ** 2)
    return (noise * amplitude * envelope).astype(jnp.bfloat16)


def plant(result, key, smallest, largest):
    shape = result.shape
    spot = [jax.random.randint(jax.random.fold_in(key, axis), (), 0, shape[axis]) for axis in range(len(shape))]
    result = result.at[tuple(spot)].set(smallest)
    longest = shape.index(max(shape))
    spot[longest] = (spot[longest] + 1) % shape[longest]
    return result.at[tuple(spot)].set(largest)


def level_of(rng, shape, shards, least, high):
    def one(dim, blocks):
        heights = jax.random.uniform(jax.random.fold_in(jax.random.fold_in(rng, 6), dim), (blocks,), jnp.float32, least / len(shards), high / len(shards))
        return jnp.repeat(jnp.exp(heights), shape[dim] // blocks).reshape((-1,) + (1,) * (len(shape) - dim - 1))

    level = one(*shards[0])
    for cut in shards[1:]:
        level = level * one(*cut)
    return level


def centred(rng, dims, scale, reach, pieces=(), kind=jnp.bfloat16):
    gain = level_of(rng, dims, pieces, -0.22, 0.18) if pieces else 1.0
    result = jax.random.normal(rng, dims, jnp.float32) * scale * gain
    return jnp.minimum(jnp.maximum(result, -reach), reach).astype(kind)


def setup_inputs(seed: int = 0, part: int = 0) -> dict:
    splits = jax.random.split(jax.random.key(seed), 6)
    part_keys = jax.random.split(jax.random.fold_in(splits[5], part), 6)
    records = draw_records(jax.random.fold_in(jax.random.fold_in(splits[5], part), 71), part)
    templates = centred(splits[1], (TEMPLATES, NSTAT, 3, TAPS), 1.0, 6.0, ((0, 16),))
    fetch_list = draw_fetch_list(jax.random.fold_in(splits[5], 71), part)
    cluster_slots = draw_cluster_slots(jax.random.fold_in(splits[5], 71), part)
    moveouts = plant(jax.random.randint(splits[4], (TEMPLATES, NSTAT), 0, MOVE), jax.random.fold_in(splits[4], 1), 0, MOVE - 1).astype(jnp.int32)
    return {"records": records, "templates": templates, "fetch_list": fetch_list, "cluster_slots": cluster_slots, "moveouts": moveouts}


def align_row(series, offset):
    return lax.dynamic_slice_in_dim(series, offset.astype(jnp.int32), OUT)

def cluster_stack(traces, kernels, shifts):
    tap_count = kernels.shape[-1]
    members = kernels.shape[0]
    stations = traces.shape[0]
    inputs_nch = traces.reshape(1, stations * 3, traces.shape[-1])
    filters = jnp.transpose(kernels, (1, 2, 0, 3)).reshape(stations * 3 * members, 1, tap_count)
    products = lax.conv_general_dilated(inputs_nch, filters, (1,), 'VALID', dimension_numbers=('NCH', 'OIH', 'NCH'), feature_group_count=stations * 3, precision=lax.Precision.HIGHEST, preferred_element_type=jnp.float32)[0]
    lag_count = products.shape[-1]
    products = products.reshape(stations, 3, members, lag_count)
    energy = lax.reduce_window(traces * traces, jnp.array(0, traces.dtype), lax.add, (1, 1, tap_count), (1, 1, 1), 'VALID')
    data_scale = jnp.sqrt(energy / tap_count + 1e-05)
    tmpl_scale = jnp.sqrt(lax.optimization_barrier(jnp.mean(kernels * kernels, axis=-1)) + 1e-05)
    normed = products / (tap_count * jnp.transpose(tmpl_scale, (1, 2, 0))[..., None] * data_scale[:, :, None, :])
    channel_sum = lax.optimization_barrier(jnp.sum(normed, axis=1))
    aligned = jax.vmap(jax.vmap(align_row))(channel_sum, shifts.T)
    return lax.optimization_barrier(jnp.sum(aligned, axis=0))

def reference(records, templates, fetch_list, cluster_slots, moveouts):
    clusters = cluster_slots.shape[0]
    group_ids = jnp.arange(clusters, dtype=jnp.int32) // CLUST
    owner_ids = cluster_slots // CAP
    within = cluster_slots % CAP
    local_ids = fetch_list[group_ids[:, None], owner_ids, within]
    station_ids = (owner_ids * STA_DEV + local_ids).astype(jnp.int32)
    kernels_all = templates.reshape(clusters, TPC, NSTAT, 3, TAPS)
    shifts_all = moveouts.reshape(clusters, TPC, NSTAT)

    def one_cluster(inputs):
        ids, kernels, shifts = inputs
        traces = jnp.take(records, ids, axis=0).astype(jnp.float32)
        return cluster_stack(traces, kernels.astype(jnp.float32), shifts)
    stacks = lax.map(one_cluster, (station_ids, kernels_all, shifts_all))
    stack = stacks.reshape(clusters * TPC, OUT)
    return (stack, lax.optimization_barrier(jnp.max(stack, axis=0)))
```

```python
import functools

import jax
import jax.numpy as jnp
from jax import lax
from jax.experimental import pallas as pl
from jax.experimental.pallas import tpu as pltpu
from jax.sharding import PartitionSpec as P

OUT = 256
LANES = 128
FINE = 16
ROWS = OUT // FINE
PACK = LANES // FINE


def push(src, dst, send, recv, peer):
    return pltpu.make_async_remote_copy(
        src_ref=src,
        dst_ref=dst,
        send_sem=send,
        recv_sem=recv,
        device_id={"tmpl": peer},
        device_id_type=pl.DeviceIdType.MESH,
    )


def each(low, high, action):
    def body(d, carry):
        action(d)
        return carry

    lax.fori_loop(low, high, body, 0)


def kernel(
    n, stations, sets, nstat, taps,
    list_hbm, slots_hbm, moves_hbm, rec_hbm, tm_hbm,
    stack_ref, peak_ref,
    list_ref, slots_ref, moves_ref, rec_ref, tm_ref, req_ref, asked, stage, rx_ref,
    hs, hl, tinv, weights, gains, turns, band, xf, windows, scales, rows_ref, lines, mine, held,
    local, s1, r1, s2, r2, s3, r3,
):
    me = lax.axis_index("tmpl")
    tm_copy = pltpu.make_async_copy(tm_hbm, tm_ref, local.at[0])
    rec_copy = pltpu.make_async_copy(rec_hbm, rec_ref, local.at[1])
    list_copy = pltpu.make_async_copy(list_hbm, list_ref, local.at[2])
    slots_copy = pltpu.make_async_copy(slots_hbm, slots_ref, local.at[3])
    moves_copy = pltpu.make_async_copy(moves_hbm, moves_ref, local.at[4])
    list_copy.start()
    rec_copy.start()
    slots_copy.start()
    moves_copy.start()
    tm_copy.start()

    rx_ref[...] = jnp.zeros_like(rx_ref)
    barrier = pltpu.get_barrier_semaphore()
    each(1, n, lambda d: pl.semaphore_signal(
        barrier, inc=1, device_id={"tmpl": lax.rem(me + d, n)},
        device_id_type=pl.DeviceIdType.MESH))

    row = lax.broadcasted_iota(jnp.int32, (8, LANES), 0)
    lane = lax.broadcasted_iota(jnp.int32, (8, LANES), 1)
    comp = jnp.where(row < 3, row, row - 3)

    def request(o):
        wanted = jnp.where(row < 3, list_ref[0, o], list_ref[1, o])
        valid = jnp.logical_and(wanted >= 0, row < 6)
        req_ref[o] = jnp.where(valid, comp * stations + wanted, -1)

    list_copy.wait()
    each(0, n, request)
    pl.semaphore_wait(barrier, n - 1)

    def ask(d):
        peer = lax.rem(me + d, n)
        return push(req_ref.at[peer], asked.at[me], s1.at[d], r1.at[d], peer)

    def give(d):
        peer = lax.rem(me + d, n)
        return push(stage.at[peer, pl.ds(0, 6)], rx_ref.at[me, pl.ds(0, 6)], s2.at[d], r2.at[d], peer)

    def tell(d):
        peer = lax.rem(me + d, n)
        return push(mine, held.at[me], s3.at[d], r3.at[d], peer)

    each(1, n, lambda d: ask(d).start())
    asked[me] = req_ref[me]
    slots_copy.wait()
    moves_copy.wait()
    tm_copy.wait()

    deep = hs.shape[1]
    pairs = sets * nstat
    lane16 = lax.broadcasted_iota(jnp.int32, (FINE, LANES), 1)
    row16 = lax.broadcasted_iota(jnp.int32, (FINE, LANES), 0)

    for c in range(3):
        for k in range(sets):
            for v in range(deep):
                end = min(taps - v * LANES, LANES)
                some = tm_ref[k, c, :, v * LANES : v * LANES + end].astype(jnp.float32)
                if end < LANES:
                    some = jnp.concatenate(
                        [some, jnp.zeros((nstat, LANES - end), jnp.float32)], axis=1)
                hs[c, v, k * nstat : (k + 1) * nstat, :] = some
        total = sum(hs[c, v] * hs[c, v] for v in range(deep))
        tscale = jnp.sqrt(jnp.sum(total, axis=1, keepdims=True) / taps + 1e-05)
        tinv[c] = jnp.broadcast_to(1.0 / (taps * tscale), (pairs, LANES))
        head = lax.broadcasted_iota(jnp.int32, (pairs, LANES), 1) >= FINE
        moved = [pltpu.roll(hs[c, v], FINE, 1) for v in range(deep)]
        for v in range(deep):
            hl[c, v] = jnp.where(head, moved[v], moved[v - 1] if v else 0.0)

    def prepare(at):
        fines = [moves_ref[(at * PACK + g) // nstat, lax.rem(at * PACK + g, nstat)] & (FINE - 1) for g in range(PACK)]
        turn = jnp.zeros((8, LANES), jnp.int32)
        for g in range(PACK):
            turn = jnp.where(lane >= g * FINE, fines[g], turn)
        turns[at] = turn
        keep = lane16 >= row16
        for c in range(3):
            gain = jnp.zeros((8, LANES), jnp.float32)
            for g in range(PACK):
                e = at * PACK + g
                turned = []
                for v in range(deep):
                    near = jnp.broadcast_to(hs[c, v, pl.ds(e, 1), :], (8, LANES))
                    far = jnp.broadcast_to(hl[c, v, pl.ds(e, 1), :], (8, LANES))
                    source = jnp.concatenate(
                        [jnp.where(row + i < fines[g], far, near) for i in range(0, FINE, 8)], axis=0)
                    turned.append(pltpu.roll(source.astype(jnp.bfloat16), 0, 1, stride=1, stride_axis=0))
                for v in range(deep):
                    block = jnp.where(keep, turned[v], turned[v - 1] if v else jnp.zeros_like(turned[0]))
                    weights[c, at, g * FINE : (g + 1) * FINE, v * LANES : (v + 1) * LANES] = block
                gain = jnp.where(
                    lane >= g * FINE, jnp.broadcast_to(tinv[c, pl.ds(e, 1), :], (8, LANES)), gain)
            gains[c, at] = gain

    each(0, pairs // PACK, prepare)
    s = lax.broadcasted_iota(jnp.int32, band.shape, 0)
    u = lax.broadcasted_iota(jnp.int32, band.shape, 1)
    band[...] = jnp.where(
        jnp.logical_and(s >= u, s < u + taps), 1.0, 0.0).astype(jnp.bfloat16)

    rec_copy.wait()
    each(1, n, lambda d: ask(d).wait())
    rows = n * 8
    depth, width = rec_ref.shape
    want = asked[...].reshape(rows, LANES)[:, :depth]
    spot = lax.broadcasted_iota(jnp.int32, (rows, depth), 1)
    onehot = jnp.where(want == spot, 1.0, 0.0).astype(jnp.bfloat16)
    picked = jnp.dot(onehot, rec_ref[...], preferred_element_type=jnp.float32)
    stage[...] = picked.reshape(n, 8, width).astype(jnp.bfloat16)
    each(1, n, lambda d: give(d).start())
    rx_ref[me] = stage[me]
    each(1, n, lambda d: give(d).wait())

    wide = windows.shape[0] // (6 * n)
    tall = rows_ref.shape[0] // (6 * n)
    block = min(rows, 128)

    def scale(i):
        at = pl.multiple_of(i * block, block)
        samples = rx_ref[pl.ds(i * (block // 8), block // 8)].reshape(block, width).astype(jnp.float32)
        for v in range(width // LANES):
            xf[v, pl.ds(at, block), :] = samples[:, v * LANES : (v + 1) * LANES]
        power = samples * samples
        high = power.astype(jnp.bfloat16)
        rest = (power - high.astype(jnp.float32)).astype(jnp.bfloat16)
        energy = jnp.dot(high, band[...], preferred_element_type=jnp.float32)
        energy += jnp.dot(rest, band[...], preferred_element_type=jnp.float32)
        inverse = lax.rsqrt(energy / taps + 1e-05)
        for v in range(band.shape[1] // LANES):
            scales[v, pl.ds(at, block), :] = inverse[:, v * LANES : (v + 1) * LANES]

    each(0, rows // block, scale)

    begin = (lane + FINE * row) & (LANES - 1)
    repeat = (lane & (FINE - 1)) + FINE * row
    inside = lane < LANES - FINE * row

    def turn_by(series, index):
        return jnp.take_along_axis(jnp.broadcast_to(series, (8, LANES)), index, axis=1)

    def unfold(o):
        for r in range(6):
            at = o * 6 + r
            parts = [turn_by(xf[v, pl.ds(o * 8 + r, 1), :], begin) for v in range(wide // 8)]
            for v, part in enumerate(parts):
                after = parts[min(v + 1, len(parts) - 1)]
                windows[pl.ds(at * wide + 8 * v, 8), :] = jnp.where(inside, part, after)
            for v in range(tall // 8):
                rows_ref[pl.ds(at * tall + 8 * v, 8), :] = turn_by(
                    scales[v, pl.ds(o * 8 + r, 1), :], repeat)

    each(0, n, unfold)

    def pick(parts):
        out = parts[0]
        for g in range(1, PACK):
            out = jnp.where(lane >= g * FINE, parts[g], out)
        return out

    def correlate(i, at, e):
        turn = turns[at]
        wraps = (lane & (FINE - 1)) < turn
        where = []
        for g in range(PACK):
            k, j = (e + g) // nstat, (e + g) % nstat
            slot = slots_ref[2 * i + k, j]
            move = moves_ref[2 * i + k, j]
            where.append((slot * 3, move >> 4))
        acc = [jnp.zeros((8, LANES), jnp.float32)] * 2
        for c in range(3):
            left = []
            for s, a in where:
                got = [windows[pl.ds((s + c) * wide + a + 8 * v, 8), :] for v in range(deep + 1)]
                left.append(jnp.concatenate(
                    [jnp.concatenate(got[v : v + 2], axis=0) for v in range(deep)], axis=1))
            left = jnp.concatenate(left, axis=0).astype(jnp.bfloat16)
            got = lax.dot_general(
                left, weights[c, at], (((1,), (1,)), ((), ())), preferred_element_type=jnp.float32)
            gain = gains[c, at]
            for h in range(2):
                product = pick([got[FINE * g + 8 * h : FINE * g + 8 * h + 8] for g in range(PACK)])
                near = pick([rows_ref[pl.ds((s + c) * tall + a + 8 * h, 8), :] for s, a in where])
                far = pick([rows_ref[pl.ds((s + c) * tall + a + 8 * h + 1, 8), :] for s, a in where])
                acc[h] = acc[h] + product * (jnp.where(wraps, far, near) * gain)
        order = (lane & (LANES - FINE)) + ((lane + turn) & (FINE - 1))
        return [jnp.take_along_axis(x, order, axis=1) for x in acc]

    def finish(k, acc):
        for h in range(2):
            x = acc[h]
            for size in (4 * FINE, 2 * FINE, FINE):
                x = x + pltpu.roll(x, size, 1)
            x = jnp.where((lane // FINE) == row, x, 0.0)
            lines[h, pl.ds(k, 1), :] = jnp.sum(x, axis=0, keepdims=True)

    tiles = 2 * nstat // PACK

    def two(i):
        sums = [[jnp.zeros((8, LANES), jnp.float32)] * 2 for _ in range(2)]
        for t in range(tiles):
            out = correlate(i, i * tiles + t, t * PACK)
            for b in range(2):
                first = max(b * nstat - t * PACK, 0)
                last = min((b + 1) * nstat - t * PACK, PACK)
                if first >= last:
                    continue
                for h in range(2):
                    x = out[h]
                    if last - first < PACK:
                        x = jnp.where(jnp.logical_and(lane >= first * FINE, lane < last * FINE), x, 0.0)
                    sums[b][h] = sums[b][h] + x
        for b in range(2):
            finish(2 * i + b, sums[b])

    each(0, sets // 2, two)
    for h in range(2):
        stack_ref[:, h * LANES : (h + 1) * LANES] = lines[h]
    best = jnp.max(stack_ref[...], axis=0, keepdims=True)
    mine[...] = best
    each(1, n, lambda d: tell(d).start())
    held[me] = best
    each(1, n, lambda d: tell(d).wait())
    peak_ref[...] = jnp.max(held[...], axis=0)


def on_device(records, templates, fetch_list, cluster_slots, moveouts):
    n = fetch_list.shape[1]
    stations, comps, width = records.shape
    sets, nstat = cluster_slots.shape
    taps = templates.shape[-1]
    deep = -(-(taps + 2 * FINE - 1) // LANES) * LANES
    most = width - OUT - taps + 1
    wide = -(-(most // FINE + ROWS + PACK * (deep // LANES - 1)) // 8) * 8
    tall = -(-(most // FINE + ROWS + 1) // 8) * 8
    used = -(-(OUT + most) // LANES) * LANES
    tiles = sets * nstat // PACK
    rec_flat = jnp.transpose(records, (1, 0, 2)).reshape(comps * stations, width)
    kernels = jnp.transpose(templates, (0, 2, 1, 3))
    vmem = pl.BlockSpec(memory_space=pltpu.VMEM)
    far = pl.BlockSpec(memory_space=pltpu.HBM)
    sems = pltpu.SemaphoreType.DMA((n,))
    stack, peak = pl.pallas_call(
        functools.partial(kernel, n, stations, sets, nstat, taps),
        out_shape=(
            jax.ShapeDtypeStruct((sets, OUT), jnp.float32),
            jax.ShapeDtypeStruct((1, OUT), jnp.float32),
        ),
        in_specs=[far] * 5,
        out_specs=(vmem, vmem),
        scratch_shapes=[
            pltpu.SMEM((fetch_list.shape[2], n), jnp.int32),
            pltpu.SMEM(cluster_slots.shape, jnp.int32),
            pltpu.SMEM(moveouts.shape, jnp.int32),
            pltpu.VMEM(rec_flat.shape, jnp.bfloat16),
            pltpu.VMEM(kernels.shape, jnp.bfloat16),
            pltpu.VMEM((n, 8, LANES), jnp.int32),
            pltpu.VMEM((n, 8, LANES), jnp.int32),
            pltpu.VMEM((n, 8, width), jnp.bfloat16),
            pltpu.VMEM((n, 8, width), jnp.bfloat16),
            pltpu.VMEM((3, deep // LANES, sets * nstat, LANES), jnp.float32),
            pltpu.VMEM((3, deep // LANES, sets * nstat, LANES), jnp.float32),
            pltpu.VMEM((3, sets * nstat, LANES), jnp.float32),
            pltpu.VMEM((3, tiles, LANES, deep), jnp.bfloat16),
            pltpu.VMEM((3, tiles, 8, LANES), jnp.float32),
            pltpu.VMEM((tiles, 8, LANES), jnp.int32),
            pltpu.VMEM((width, used), jnp.bfloat16),
            pltpu.VMEM((width // LANES, n * 8, LANES), jnp.float32),
            pltpu.VMEM((n * 6 * wide, LANES), jnp.float32),
            pltpu.VMEM((used // LANES, n * 8, LANES), jnp.float32),
            pltpu.VMEM((n * 6 * tall, LANES), jnp.float32),
            pltpu.VMEM((2, sets, LANES), jnp.float32),
            pltpu.VMEM((1, OUT), jnp.float32),
            pltpu.VMEM((n, 1, OUT), jnp.float32),
            pltpu.SemaphoreType.DMA((5,)),
            sems, sems, sems, sems, sems, sems,
        ],
        compiler_params=pltpu.CompilerParams(
            collective_id=0, has_side_effects=True, vmem_limit_bytes=60 << 20
        ),
        name="network_stack",
    )(jnp.transpose(fetch_list[0]), cluster_slots, moveouts, rec_flat, kernels)
    return stack, peak.reshape(OUT)


def solution(mesh):
    placed = (
        P(("groups", "tmpl"), None, None),
        P("tmpl", None, None, None),
        P("tmpl", None, None),
        P("tmpl", None),
        P("tmpl", None),
    )
    return jax.shard_map(
        on_device,
        mesh=mesh,
        in_specs=placed,
        out_specs=(P(("groups", "tmpl"), None), P("groups")),
        check_vma=False,
    )
```

```python
import functools

import jax
import jax.numpy as jnp
from jax import lax
from jax.experimental import pallas as pl
from jax.experimental.pallas import tpu as pltpu
from jax.sharding import PartitionSpec as P

OUT = 256
LANES = 128
FINE = 16
ROWS = OUT // FINE
PACK = LANES // FINE
UNROLL = 15
SPLIT = 8


def push(src, dst, send, recv, peer):
    return pltpu.make_async_remote_copy(
        src_ref=src,
        dst_ref=dst,
        send_sem=send,
        recv_sem=recv,
        device_id={"tmpl": peer},
        device_id_type=pl.DeviceIdType.MESH,
    )


def each(low, high, action):
    def body(d, carry):
        action(d)
        return carry

    lax.fori_loop(low, high, body, 0)


def kernel(
    n, stations, sets, nstat, taps,
    list_hbm, slots_hbm, moves_hbm, rec_hbm, tm_hbm,
    stack_ref, peak_ref,
    list_ref, slots_ref, moves_ref, rec_ref, tm_ref, req_ref, asked, want_ref, stage, rx_ref,
    hs, hl, tinv, weights, gains, turns, band, shift, repeat, windows, scales, first, xf, chan, lines, mine, held,
    local, s1, r1, s2, r2, s3, r3,
):
    me = lax.axis_index("tmpl")
    tm_copy = pltpu.make_async_copy(tm_hbm, tm_ref, local.at[0])
    rec_copy = pltpu.make_async_copy(rec_hbm, rec_ref, local.at[1])
    list_copy = pltpu.make_async_copy(list_hbm, list_ref, local.at[2])
    slots_copy = pltpu.make_async_copy(slots_hbm, slots_ref, local.at[3])
    moves_copy = pltpu.make_async_copy(moves_hbm, moves_ref, local.at[4])
    list_copy.start()
    rec_copy.start()
    slots_copy.start()
    moves_copy.start()
    tm_copy.start()

    barrier = pltpu.get_barrier_semaphore()
    each(1, n, lambda d: pl.semaphore_signal(
        barrier, inc=1, device_id={"tmpl": lax.rem(me + d, n)},
        device_id_type=pl.DeviceIdType.MESH))

    row = lax.broadcasted_iota(jnp.int32, (8, LANES), 0)
    lane = lax.broadcasted_iota(jnp.int32, (8, LANES), 1)
    pair = lax.broadcasted_iota(jnp.int32, (2, LANES), 0)

    def request(o):
        req_ref[o] = jnp.where(pair < 1, list_ref[0, o], list_ref[1, o])

    list_copy.wait()
    each(0, n, request)
    pl.semaphore_wait(barrier, n - 1)

    def ask(d):
        peer = lax.rem(me + d, n)
        return push(req_ref.at[peer], asked.at[d], s1, r1, peer)

    def give(c, d):
        peer = lax.rem(me + d, n)
        pair = pl.ds(2 * c, 2)
        return push(stage.at[peer, pair], rx_ref.at[d, pair], s2.at[c], r2.at[c], peer)

    def tell(d):
        peer = lax.rem(me + d, n)
        return push(mine, held.at[d], s3, r3, peer)

    others = pl.ds(1, n - 1)

    def asks():
        return push(req_ref.at[others], asked.at[others], s1, r1, lax.rem(me + 1, n))

    def gives(c):
        pair = pl.ds(2 * c, 2)
        return push(stage.at[others, pair], rx_ref.at[others, pair], s2.at[c], r2.at[c], lax.rem(me + 1, n))

    def tells():
        return push(held.at[others], held.at[others], s3, r3, lax.rem(me + 1, n))

    each(1, n, lambda d: ask(d).start())
    asked[0] = req_ref[me]

    deep = hs.shape[1]
    pairs = sets * nstat
    lane16 = lax.broadcasted_iota(jnp.int32, (FINE, LANES), 1)
    row16 = lax.broadcasted_iota(jnp.int32, (FINE, LANES), 0)
    wide = windows.shape[0] // (6 * n)
    tall = scales.shape[0] // (6 * n)
    width = rec_ref.shape[1]

    def series():
        for c in range(3):
            for k in range(sets):
                for v in range(deep):
                    end = min(taps - v * LANES, LANES)
                    some = tm_ref[k, c, :, v * LANES : v * LANES + end].astype(jnp.float32)
                    if end < LANES:
                        some = jnp.concatenate(
                            [some, jnp.zeros((nstat, LANES - end), jnp.float32)], axis=1)
                    hs[c, v, k * nstat : (k + 1) * nstat, :] = some
            total = sum(hs[c, v] * hs[c, v] for v in range(deep))
            tscale = jnp.sqrt(jnp.sum(total, axis=1, keepdims=True) / taps + 1e-05)
            tinv[c] = jnp.broadcast_to(1.0 / (taps * tscale), (pairs, LANES))
            head = lax.broadcasted_iota(jnp.int32, (pairs, LANES), 1) >= FINE
            moved = [pltpu.roll(hs[c, v], FINE, 1) for v in range(deep)]
            for v in range(deep):
                hl[c, v] = jnp.where(head, moved[v], moved[v - 1] if v else 0.0)

    def prepare(at):
        fines = []
        for g in range(PACK):
            e = at * PACK + g
            k, j = e // nstat, lax.rem(e, nstat)
            slot, move = slots_ref[k, j], moves_ref[k, j]
            place = lax.rem(me - (slot >> 1) + n, n) * 2 + (slot & 1)
            first[0, e] = place * wide + (move >> 4)
            first[1, e] = place * tall + (move >> 4)
            fines.append(move & (FINE - 1))
        turn = jnp.zeros((8, LANES), jnp.int32)
        for g in range(PACK):
            turn = jnp.where(lane >= g * FINE, fines[g], turn)
        turns[at] = turn
        keep = lane16 >= row16
        for c in range(3):
            gain = jnp.zeros((8, LANES), jnp.float32)
            for g in range(PACK):
                e = at * PACK + g
                turned = []
                for v in range(deep):
                    near = jnp.broadcast_to(hs[c, v, pl.ds(e, 1), :], (8, LANES))
                    far = jnp.broadcast_to(hl[c, v, pl.ds(e, 1), :], (8, LANES))
                    source = jnp.concatenate(
                        [jnp.where(row + i < fines[g], far, near) for i in range(0, FINE, 8)], axis=0)
                    turned.append(pltpu.roll(source.astype(jnp.bfloat16), 0, 1, stride=1, stride_axis=0))
                for v in range(deep):
                    block = jnp.where(keep, turned[v], turned[v - 1] if v else jnp.zeros_like(turned[0]))
                    weights[c, at, g * FINE : (g + 1) * FINE, v * LANES : (v + 1) * LANES] = block
                gain = jnp.where(
                    lane >= g * FINE, jnp.broadcast_to(tinv[c, pl.ds(e, 1), :], (8, LANES)), gain)
            gains[c, at] = gain

    def constants():
        s = lax.broadcasted_iota(jnp.int32, band.shape, 0)
        u = lax.broadcasted_iota(jnp.int32, band.shape, 1)
        band[...] = jnp.where(
            jnp.logical_and(s >= u, s < u + taps), 1.0, 0.0).astype(jnp.bfloat16)
        s = lax.broadcasted_iota(jnp.int32, (2 * LANES, LANES), 0)
        u = lax.broadcasted_iota(jnp.int32, (2 * LANES, LANES), 1)
        for i in range(PACK):
            span = slice(i * LANES, (i + 1) * LANES)
            shift[:, span] = jnp.where(s == u + FINE * i, 1.0, 0.0).astype(jnp.bfloat16)
            same = (s & (LANES - 1)) == (u & (FINE - 1)) + FINE * i
            repeat[:, span] = jnp.where(same, 1.0, 0.0).astype(jnp.bfloat16)

    tm_copy.wait()
    slots_copy.wait()
    moves_copy.wait()
    series()
    each(0, SPLIT, prepare)
    rec_copy.wait()
    asks().wait_recv()
    rows = n * 8
    depth = rec_ref.shape[0]

    comp = row >> 1

    def spell(g):
        d = lax.rem(me - g + n, n)
        wanted = jnp.where((row & 1) == 0, asked[d, 0:1, :], asked[d, 1:2, :])
        valid = jnp.logical_and(wanted >= 0, row < 6)
        want_ref[g] = jnp.where(valid, comp * stations + wanted, -1)

    def gather(i):
        for g in range(16):
            spell(i * 16 + g)
        want = want_ref[pl.ds(i * 16, 16)].reshape(LANES, LANES)[:, :depth]
        spot = lax.broadcasted_iota(jnp.int32, (LANES, depth), 1)
        onehot = jnp.where(want == spot, 1.0, 0.0).astype(jnp.bfloat16)
        picked = jnp.dot(onehot, rec_ref[...], preferred_element_type=jnp.float32)
        stage[pl.ds(i * 16, 16)] = picked.reshape(16, 8, width).astype(jnp.bfloat16)

    each(0, n // 16, gather)
    for c in range(3):
        each(1, n, lambda d: give(c, d).start())
    rx_ref[0] = stage[me]
    constants()
    each(SPLIT, pairs // PACK, prepare)

    def halves(x):
        high = x.astype(jnp.bfloat16)
        return high, (x - high.astype(jnp.float32)).astype(jnp.bfloat16)

    def unfold(c, i):
        size = 32
        for d in range(16):
            some = rx_ref[i * 16 + d, 2 * c : 2 * c + 2, :].astype(jnp.float32)
            for v in range(width // LANES):
                xf[v, 2 * d : 2 * d + 2, :] = some[:, v * LANES : (v + 1) * LANES]
        raw = jnp.concatenate([xf[v] for v in range(width // LANES)], axis=1)
        high, low = halves(raw * raw)
        samples = raw.astype(jnp.bfloat16)
        pieces = [samples[:, v * LANES : (v + 1) * LANES] for v in range(wide // 8)]
        pieces.append(jnp.zeros_like(pieces[0]))
        left = jnp.concatenate(
            [jnp.concatenate(pieces[v : v + 2], axis=1) for v in range(wide // 8)], axis=0)
        energy = jnp.dot(
            jnp.concatenate([high, low], axis=0), band[...], preferred_element_type=jnp.float32)
        out = jnp.dot(left, shift[...], preferred_element_type=jnp.float32)
        inverse = lax.rsqrt((energy[:size] + energy[size:]) / taps + 1e-05)
        high, low = halves(inverse)
        spread = jnp.concatenate(
            [jnp.concatenate([x[:, v * LANES : (v + 1) * LANES] for x in (high, low)], axis=1)
             for v in range(tall // 8)], axis=0)
        out2 = jnp.dot(spread, repeat[...], preferred_element_type=jnp.float32)
        base = (c * n + i * 16) * 2
        for target, value, count in ((windows, out, wide), (scales, out2, tall)):
            for v in range(count // 8):
                for x in range(PACK):
                    for q in range(0, size, 8):
                        target[pl.ds((base + q) * count + 8 * v + x, 8, stride=count), :] = (
                            value[v * size + q : v * size + q + 8, x * LANES : (x + 1) * LANES])

    def pick(parts):
        out = parts[0]
        for g in range(1, PACK):
            out = jnp.where(lane >= g * FINE, parts[g], out)
        return out

    def correlate(c, at):
        wraps = (lane & (FINE - 1)) < turns[at]
        starts = [[first[b, at * PACK + g] for g in range(PACK)] for b in range(2)]
        left = []
        for a in starts[0]:
            got = [windows[pl.ds(a + (c * 2 * n * wide + 8 * v), 8), :] for v in range(deep + 1)]
            left.append(jnp.concatenate(
                [jnp.concatenate(got[v : v + 2], axis=0) for v in range(deep)], axis=1))
        left = jnp.concatenate(left, axis=0).astype(jnp.bfloat16)
        got = lax.dot_general(
            left, weights[c, at], (((1,), (1,)), ((), ())), preferred_element_type=jnp.float32)
        gain = gains[c, at]
        for h in range(2):
            product = pick([got[FINE * g + 8 * h : FINE * g + 8 * h + 8] for g in range(PACK)])
            near = pick([scales[pl.ds(a + (c * 2 * n * tall + 8 * h), 8), :] for a in starts[1]])
            far = pick([scales[pl.ds(a + (c * 2 * n * tall + 8 * h + 1), 8), :] for a in starts[1]])
            term = product * (jnp.where(wraps, far, near) * gain)
            chan[at, h] = chan[at, h] + term if c else term

    def component(c):
        gives(c).wait_recv()
        each(0, n // 16, lambda i: unfold(c, i))
        each(0, pairs // PACK // UNROLL, lambda i: [correlate(c, i * UNROLL + t) for t in range(UNROLL)] and None)

    for c in range(3):
        component(c)

    sums = [[jnp.zeros((8, LANES), jnp.float32)] * 2 for _ in range(sets)]
    for at in range(pairs // PACK):
        order = (lane & (LANES - FINE)) + ((lane + turns[at]) & (FINE - 1))
        for h in range(2):
            out = jnp.take_along_axis(chan[at, h], order, axis=1)
            for k in range(at * PACK // nstat, ((at + 1) * PACK - 1) // nstat + 1):
                low = max(k * nstat - at * PACK, 0)
                high = min((k + 1) * nstat - at * PACK, PACK)
                x = out
                if high - low < PACK:
                    x = jnp.where(jnp.logical_and(lane >= low * FINE, lane < high * FINE), x, 0.0)
                sums[k][h] = sums[k][h] + x
    for h in range(2):
        done = []
        for k in range(sets):
            x = sums[k][h]
            for size in (4 * FINE, 2 * FINE, FINE):
                x = x + pltpu.roll(x, size, 1)
            x = jnp.where((lane // FINE) == row, x, 0.0)
            done.append(jnp.sum(x, axis=0, keepdims=True))
        lines[h] = jnp.concatenate(done, axis=0)

    stack = jnp.concatenate([lines[0], lines[1]], axis=1)
    best = jnp.max(stack, axis=0, keepdims=True)
    mine[...] = best
    each(1, n, lambda d: tell(d).start())
    stack_ref[...] = stack
    held[0] = best
    tells().wait_recv()
    peak_ref[...] = jnp.max(held[...], axis=0)
    asks().wait_send()
    for c in range(3):
        gives(c).wait_send()
    tells().wait_send()


def on_device(records, templates, fetch_list, cluster_slots, moveouts):
    n = fetch_list.shape[1]
    stations, comps, width = records.shape
    sets, nstat = cluster_slots.shape
    taps = templates.shape[-1]
    deep = -(-(taps + 2 * FINE - 1) // LANES) * LANES
    most = width - OUT - taps + 1
    wide = -(-(most // FINE + ROWS + PACK * (deep // LANES - 1)) // 8) * 8
    tall = -(-(most // FINE + ROWS + 1) // 8) * 8
    used = -(-(OUT + most) // LANES) * LANES
    tiles = sets * nstat // PACK
    rec_flat = jnp.transpose(records, (1, 0, 2)).reshape(comps * stations, width)
    kernels = jnp.transpose(templates, (0, 2, 1, 3))
    vmem = pl.BlockSpec(memory_space=pltpu.VMEM)
    far = pl.BlockSpec(memory_space=pltpu.HBM)
    one = pltpu.SemaphoreType.DMA
    trio = pltpu.SemaphoreType.DMA((3,))
    stack, peak = pl.pallas_call(
        functools.partial(kernel, n, stations, sets, nstat, taps),
        out_shape=(
            pltpu.VMEM((sets, OUT), jnp.float32),
            pltpu.VMEM((1, OUT), jnp.float32),
        ),
        in_specs=[far] * 5,
        out_specs=(vmem, vmem),
        scratch_shapes=[
            pltpu.SMEM((fetch_list.shape[2], n), jnp.int32),
            pltpu.SMEM(cluster_slots.shape, jnp.int32),
            pltpu.SMEM(moveouts.shape, jnp.int32),
            pltpu.VMEM(rec_flat.shape, jnp.bfloat16),
            pltpu.VMEM(kernels.shape, jnp.bfloat16),
            pltpu.VMEM((n, 2, LANES), jnp.int32),
            pltpu.VMEM((n, 2, LANES), jnp.int32),
            pltpu.VMEM((n, 8, LANES), jnp.int32),
            pltpu.VMEM((n, 8, width), jnp.bfloat16),
            pltpu.VMEM((n, 8, width), jnp.bfloat16),
            pltpu.VMEM((3, deep // LANES, sets * nstat, LANES), jnp.float32),
            pltpu.VMEM((3, deep // LANES, sets * nstat, LANES), jnp.float32),
            pltpu.VMEM((3, sets * nstat, LANES), jnp.float32),
            pltpu.VMEM((3, tiles, LANES, deep), jnp.bfloat16),
            pltpu.VMEM((3, tiles, 8, LANES), jnp.float32),
            pltpu.VMEM((tiles, 8, LANES), jnp.int32),
            pltpu.VMEM((width, used), jnp.bfloat16),
            pltpu.VMEM((2 * LANES, PACK * LANES), jnp.bfloat16),
            pltpu.VMEM((2 * LANES, PACK * LANES), jnp.bfloat16),
            pltpu.VMEM((n * 6 * wide, LANES), jnp.float32),
            pltpu.VMEM((n * 6 * tall, LANES), jnp.float32),
            pltpu.SMEM((2, sets * nstat), jnp.int32),
            pltpu.VMEM((width // LANES, 32, LANES), jnp.float32),
            pltpu.VMEM((tiles, 2, 8, LANES), jnp.float32),
            pltpu.VMEM((2, sets, LANES), jnp.float32),
            pltpu.VMEM((1, OUT), jnp.float32),
            pltpu.VMEM((n, 1, OUT), jnp.float32),
            pltpu.SemaphoreType.DMA((5,)),
            one, one, trio, trio, one, one,
        ],
        compiler_params=pltpu.CompilerParams(
            collective_id=0, has_side_effects=True, vmem_limit_bytes=60 << 20
        ),
        name="network_stack",
    )(jnp.transpose(fetch_list[0]), cluster_slots, moveouts, rec_flat, kernels)
    return stack, peak.reshape(OUT)


def solution(mesh):
    placed = (
        P(("groups", "tmpl"), None, None),
        P("tmpl", None, None, None),
        P("tmpl", None, None),
        P("tmpl", None),
        P("tmpl", None),
    )
    return jax.shard_map(
        on_device,
        mesh=mesh,
        in_specs=placed,
        out_specs=(P(("groups", "tmpl"), None), P("groups")),
        check_vma=False,
    )
```

```python
import functools

import jax
import numpy as np
import jax.numpy as jnp
from jax import lax
from jax.experimental import pallas as pl
from jax.experimental.pallas import tpu as pltpu
from jax.sharding import PartitionSpec as P

OUT = 256
LANES = 128
FINE = 16
ROWS = OUT // FINE
PACK = LANES // FINE
SPLIT = 8


def push(src, dst, send, recv, peer):
    return pltpu.make_async_remote_copy(
        src_ref=src,
        dst_ref=dst,
        send_sem=send,
        recv_sem=recv,
        device_id={"tmpl": peer},
        device_id_type=pl.DeviceIdType.MESH,
    )


def each(low, high, action):
    if high - low == 1:
        action(low)
        return
    if low == 1 and high == 16:
        for d in (8, 9, 7, 10, 6, 11, 5, 12, 4, 13, 3, 14, 2, 15, 1):
            action(d)
        return

    def body(d, carry):
        action(d)
        return carry

    lax.fori_loop(low, high, body, 0)


def kernel(
    n, stations, sets, nstat, taps,
    list_hbm, slots_hbm, moves_hbm, rec_hbm, tm_hbm, band_hbm, shift_hbm, repeat_hbm,
    stack_ref, peak_ref,
    list_ref, slots_ref, moves_ref, rec_ref, tm_ref, req_ref, asked, want_ref, stage, rx_ref,
    hs, hl, tinv, weights, gains, turns, band, shift, repeat, windows, scales, first, xf, lines, mine, held,
    local, s1, r1, s2, r2, s3, r3,
):
    me = lax.axis_index("tmpl")
    tm_copy = pltpu.make_async_copy(tm_hbm, tm_ref, local.at[0])
    rec_copy = pltpu.make_async_copy(rec_hbm, rec_ref, local.at[1])
    list_copy = pltpu.make_async_copy(list_hbm, list_ref, local.at[2])
    slots_copy = pltpu.make_async_copy(slots_hbm, slots_ref, local.at[3])
    moves_copy = pltpu.make_async_copy(moves_hbm, moves_ref, local.at[4])
    list_copy.start()
    rec_copy.start()
    slots_copy.start()
    moves_copy.start()
    tm_copy.start()
    fixed = [
        pltpu.make_async_copy(band_hbm, band, local.at[5]),
        pltpu.make_async_copy(shift_hbm, shift, local.at[6]),
        pltpu.make_async_copy(repeat_hbm, repeat, local.at[7]),
    ]
    for copy in fixed:
        copy.start()

    barrier = pltpu.get_barrier_semaphore()
    each(1, n, lambda d: pl.semaphore_signal(
        barrier, inc=1, device_id={"tmpl": lax.rem(me + d, n)},
        device_id_type=pl.DeviceIdType.MESH))

    row = lax.broadcasted_iota(jnp.int32, (8, LANES), 0)
    lane = lax.broadcasted_iota(jnp.int32, (8, LANES), 1)
    pair = lax.broadcasted_iota(jnp.int32, (2, LANES), 0)

    def request(o):
        req_ref[o] = jnp.where(pair < 1, list_ref[0, o], list_ref[1, o])

    list_copy.wait()
    each(0, n, request)
    pl.semaphore_wait(barrier, n - 1)

    def ask(d):
        peer = lax.rem(me + d, n)
        return push(req_ref.at[peer], asked.at[d], s1, r1, peer)

    def give(d):
        peer = lax.rem(me + d, n)
        return push(stage.at[peer, pl.ds(0, 6)], rx_ref.at[d, pl.ds(0, 6)], s2, r2, peer)

    def tell(d):
        peer = lax.rem(me + d, n)
        return push(mine, held.at[d], s3, r3, peer)

    others = pl.ds(1, n - 1)

    def asks():
        return push(req_ref.at[others], asked.at[others], s1, r1, lax.rem(me + 1, n))

    def gives():
        six = pl.ds(0, 6)
        return push(stage.at[others, six], rx_ref.at[others, six], s2, r2, lax.rem(me + 1, n))

    def tells():
        return push(held.at[others], held.at[others], s3, r3, lax.rem(me + 1, n))

    each(1, n, lambda d: ask(d).start())
    asked[0] = req_ref[me]

    deep = hs.shape[1]
    pairs = sets * nstat
    lane16 = lax.broadcasted_iota(jnp.int32, (FINE, LANES), 1)
    row16 = lax.broadcasted_iota(jnp.int32, (FINE, LANES), 0)
    wide = windows.shape[0] // (6 * n) - 1
    tall = scales.shape[0] // (6 * n) - 1
    width = rec_ref.shape[1]

    def halves(x):
        high = x.astype(jnp.bfloat16)
        return high, (x - high.astype(jnp.float32)).astype(jnp.bfloat16)

    def series():
        for c in range(3):
            for k in range(sets):
                for v in range(deep):
                    end = min(taps - v * LANES, LANES)
                    some = tm_ref[k, c, :, v * LANES : v * LANES + end].astype(jnp.float32)
                    if end < LANES:
                        some = jnp.concatenate(
                            [some, jnp.zeros((nstat, LANES - end), jnp.float32)], axis=1)
                    hs[c, v, k * nstat : (k + 1) * nstat, :] = some
            power = jnp.concatenate([p for v in range(deep) for p in halves(hs[c, v] * hs[c, v])], axis=1)
            ones = jnp.ones((power.shape[1], LANES), jnp.bfloat16)
            total = jnp.dot(power, ones, preferred_element_type=jnp.float32)
            tinv[c] = 1.0 / (taps * jnp.sqrt(total / taps + 1e-05))
            head = lax.broadcasted_iota(jnp.int32, (pairs, LANES), 1) >= FINE
            moved = [
                pltpu.roll(hs[c, v].astype(jnp.bfloat16), FINE, 1).astype(jnp.float32) for v in range(deep)]
            for v in range(deep):
                hl[c, v] = jnp.where(head, moved[v], moved[v - 1] if v else 0.0)

    def prepare(at):
        fines = []
        for g in range(PACK):
            e = at * PACK + g
            k, j = e // nstat, lax.rem(e, nstat)
            slot, move = slots_ref[k, j], moves_ref[k, j]
            place = lax.rem(me - (slot >> 1) + n, n) * 6 + (slot & 1)
            first[0, e] = place * (wide + 1) + (move >> 4)
            first[1, e] = place * (tall + 1) + (move >> 4)
            fines.append(move & (FINE - 1))
        turn = jnp.zeros((8, LANES), jnp.int32)
        for g in range(PACK):
            turn = jnp.where(lane >= g * FINE, fines[g], turn)
        turns[at] = turn
        keep = lane16 >= row16
        for c in range(3):
            gain = jnp.zeros((8, LANES), jnp.float32)
            for g in range(PACK):
                e = at * PACK + g
                turned = []
                for v in range(deep):
                    near = jnp.broadcast_to(hs[c, v, pl.ds(e, 1), :], (8, LANES))
                    far = jnp.broadcast_to(hl[c, v, pl.ds(e, 1), :], (8, LANES))
                    source = jnp.concatenate(
                        [jnp.where(row + i < fines[g], far, near) for i in range(0, FINE, 8)], axis=0)
                    turned.append(pltpu.roll(source.astype(jnp.bfloat16), 0, 1, stride=1, stride_axis=0))
                for v in range(deep):
                    block = jnp.where(keep, turned[v], turned[v - 1] if v else jnp.zeros_like(turned[0]))
                    weights[c, at, g * FINE : (g + 1) * FINE, v * LANES : (v + 1) * LANES] = block
                gain = jnp.where(
                    lane >= g * FINE, jnp.broadcast_to(tinv[c, pl.ds(e, 1), :], (8, LANES)), gain)
            gains[c, at] = gain

    tm_copy.wait()
    slots_copy.wait()
    moves_copy.wait()
    series()
    each(0, SPLIT, prepare)
    rec_copy.wait()
    asks().wait_recv()
    rows = n * 8
    depth = rec_ref.shape[0]

    comp = row >> 1

    def spell(g):
        d = lax.rem(me - g + n, n)
        wanted = jnp.where((row & 1) == 0, asked[d, 0:1, :], asked[d, 1:2, :])
        valid = jnp.logical_and(wanted >= 0, row < 6)
        want_ref[g] = jnp.where(valid, comp * stations + wanted, -1)

    def gather(i):
        for g in range(16):
            spell(i * 16 + g)
        want = want_ref[pl.ds(i * 16, 16)].reshape(LANES, LANES)[:, :depth]
        spot = lax.broadcasted_iota(jnp.int32, (LANES, depth), 1)
        onehot = jnp.where(want == spot, 1.0, 0.0).astype(jnp.bfloat16)
        picked = jnp.dot(onehot, rec_ref[...], preferred_element_type=jnp.float32)
        stage[pl.ds(i * 16, 16)] = picked.reshape(16, 8, width).astype(jnp.bfloat16)

    each(0, n // 16, gather)
    each(1, n, lambda d: give(d).start())
    rx_ref[0] = stage[me]
    each(SPLIT, pairs // PACK, prepare)

    def unfold(i):
        size = 96
        for d in range(16):
            some = rx_ref[i * 16 + d].astype(jnp.float32)
            for v in range(width // LANES):
                xf[v, 6 * d : 6 * d + 6, :] = some[:6, v * LANES : (v + 1) * LANES]
        raw = jnp.concatenate([xf[v] for v in range(width // LANES)], axis=1)
        high, low = halves(raw * raw)
        samples = raw.astype(jnp.bfloat16)
        pieces = [samples[:, v * LANES : (v + 1) * LANES] for v in range(wide // 8)]
        pieces.append(jnp.zeros_like(pieces[0]))
        left = jnp.concatenate(
            [jnp.concatenate(pieces[v : v + 2], axis=1) for v in range(wide // 8)], axis=0)
        energy = jnp.dot(
            jnp.concatenate([high, low], axis=0), band[...], preferred_element_type=jnp.float32)
        out = jnp.dot(left, shift[...], preferred_element_type=jnp.float32)
        inverse = lax.rsqrt((energy[:size] + energy[size:]) / taps + 1e-05)
        high, low = halves(inverse)
        spread = jnp.concatenate(
            [jnp.concatenate([x[:, v * LANES : (v + 1) * LANES] for x in (high, low)], axis=1)
             for v in range(tall // 8)], axis=0)
        out2 = jnp.dot(spread, repeat[...], preferred_element_type=jnp.float32)
        base = i * size
        for target, value, count in ((windows, out, wide), (scales, out2, tall)):
            for v in range(count // 8):
                for x in range(PACK):
                    for q in range(0, size, 8):
                        target[pl.ds((base + q) * (count + 1) + 8 * v + x, 8, stride=count + 1), :] = (
                            value[v * size + q : v * size + q + 8, x * LANES : (x + 1) * LANES])

    def pick(parts):
        out = parts[0]
        for g in range(1, PACK):
            out = jnp.where(lane >= g * FINE, parts[g], out)
        return out

    def correlate(c, at):
        wraps = (lane & (FINE - 1)) < turns[at]
        starts = [[first[b, at * PACK + g] for g in range(PACK)] for b in range(2)]
        left = []
        for a in starts[0]:
            got = [windows[pl.ds(a + 2 * c * (wide + 1) + 8 * v, 8), :] for v in range(deep + 1)]
            left.append(jnp.concatenate(
                [jnp.concatenate(got[v : v + 2], axis=0) for v in range(deep)], axis=1))
        left = jnp.concatenate(left, axis=0).astype(jnp.bfloat16)
        got = lax.dot_general(
            left, weights[c, at], (((1,), (1,)), ((), ())), preferred_element_type=jnp.float32)
        gain = gains[c, at]
        for h in range(2):
            product = pick([got[FINE * g + 8 * h : FINE * g + 8 * h + 8] for g in range(PACK)])
            near = pick([scales[pl.ds(a + 2 * c * (tall + 1) + 8 * h, 8), :] for a in starts[1]])
            far = pick([scales[pl.ds(a + 2 * c * (tall + 1) + 8 * h + 1, 8), :] for a in starts[1]])
            term = product * (jnp.where(wraps, far, near) * gain)
            yield term

    for copy in fixed:
        copy.wait()
    gives().wait_recv()
    each(0, n // 16, unfold)
    sums = [[jnp.zeros((8, LANES), jnp.float32)] * 2 for _ in range(sets)]
    for at in range(pairs // PACK):
        order = (lane & (LANES - FINE)) + ((lane + turns[at]) & (FINE - 1))
        terms = [list(correlate(c, at)) for c in range(3)]
        for h in range(2):
            total = terms[0][h] + terms[1][h] + terms[2][h]
            out = jnp.take_along_axis(total, order, axis=1)
            for k in range(at * PACK // nstat, ((at + 1) * PACK - 1) // nstat + 1):
                low = max(k * nstat - at * PACK, 0)
                high = min((k + 1) * nstat - at * PACK, PACK)
                x = out
                if high - low < PACK:
                    x = jnp.where(jnp.logical_and(lane >= low * FINE, lane < high * FINE), x, 0.0)
                sums[k][h] = sums[k][h] + x
    for h in range(2):
        done = []
        for k in range(sets):
            x = sums[k][h]
            for size in (4 * FINE, 2 * FINE, FINE):
                x = x + pltpu.roll(x, size, 1)
            x = jnp.where((lane // FINE) == row, x, 0.0)
            done.append(jnp.sum(x, axis=0, keepdims=True))
        lines[h] = jnp.concatenate(done, axis=0)

    stack = jnp.concatenate([lines[0], lines[1]], axis=1)
    best = jnp.max(stack, axis=0, keepdims=True)
    mine[...] = best
    each(1, n, lambda d: tell(d).start())
    stack_ref[...] = stack
    held[0] = best
    tells().wait_recv()
    peak_ref[...] = jnp.max(held[...], axis=0)
    asks().wait_send()
    gives().wait_send()
    tells().wait_send()


def masks(taps, width, used):
    s, u = np.arange(width)[:, None], np.arange(used)[None]
    band = (s >= u) & (s < u + taps)
    s, u = np.arange(2 * LANES)[:, None], np.arange(PACK * LANES)[None]
    block, lane = u // LANES, u % LANES
    shift = s == lane + FINE * block
    repeat = s % LANES == lane % FINE + FINE * block
    return [jnp.asarray(x.astype(jnp.bfloat16)) for x in (band, shift, repeat)]


def on_device(records, templates, fetch_list, cluster_slots, moveouts):
    n = fetch_list.shape[1]
    stations, comps, width = records.shape
    sets, nstat = cluster_slots.shape
    taps = templates.shape[-1]
    deep = -(-(taps + 2 * FINE - 1) // LANES) * LANES
    most = width - OUT - taps + 1
    wide = -(-(most // FINE + ROWS + PACK * (deep // LANES - 1)) // 8) * 8
    tall = -(-(most // FINE + ROWS + 1) // 8) * 8
    used = -(-(OUT + most) // LANES) * LANES
    tiles = sets * nstat // PACK
    rec_flat = jnp.transpose(records, (1, 0, 2)).reshape(comps * stations, width)
    kernels = jnp.transpose(templates, (0, 2, 1, 3))
    vmem = pl.BlockSpec(memory_space=pltpu.VMEM)
    far = pl.BlockSpec(memory_space=pltpu.HBM)
    one = pltpu.SemaphoreType.DMA
    stack, peak = pl.pallas_call(
        functools.partial(kernel, n, stations, sets, nstat, taps),
        out_shape=(
            pltpu.VMEM((sets, OUT), jnp.float32),
            pltpu.VMEM((1, OUT), jnp.float32),
        ),
        in_specs=[far] * 8,
        out_specs=(vmem, vmem),
        scratch_shapes=[
            pltpu.SMEM((fetch_list.shape[2], n), jnp.int32),
            pltpu.SMEM(cluster_slots.shape, jnp.int32),
            pltpu.SMEM(moveouts.shape, jnp.int32),
            pltpu.VMEM(rec_flat.shape, jnp.bfloat16),
            pltpu.VMEM(kernels.shape, jnp.bfloat16),
            pltpu.VMEM((n, 2, LANES), jnp.int32),
            pltpu.VMEM((n, 2, LANES), jnp.int32),
            pltpu.VMEM((n, 8, LANES), jnp.int32),
            pltpu.VMEM((n, 8, width), jnp.bfloat16),
            pltpu.VMEM((n, 8, width), jnp.bfloat16),
            pltpu.VMEM((3, deep // LANES, sets * nstat, LANES), jnp.float32),
            pltpu.VMEM((3, deep // LANES, sets * nstat, LANES), jnp.float32),
            pltpu.VMEM((3, sets * nstat, LANES), jnp.float32),
            pltpu.VMEM((3, tiles, LANES, deep), jnp.bfloat16),
            pltpu.VMEM((3, tiles, 8, LANES), jnp.float32),
            pltpu.VMEM((tiles, 8, LANES), jnp.int32),
            pltpu.VMEM((width, used), jnp.bfloat16),
            pltpu.VMEM((2 * LANES, PACK * LANES), jnp.bfloat16),
            pltpu.VMEM((2 * LANES, PACK * LANES), jnp.bfloat16),
            pltpu.VMEM((n * 6 * (wide + 1), LANES), jnp.float32),
            pltpu.VMEM((n * 6 * (tall + 1), LANES), jnp.float32),
            pltpu.SMEM((2, sets * nstat), jnp.int32),
            pltpu.VMEM((width // LANES, 96, LANES), jnp.float32),
            pltpu.VMEM((2, sets, LANES), jnp.float32),
            pltpu.VMEM((1, OUT), jnp.float32),
            pltpu.VMEM((n, 1, OUT), jnp.float32),
            pltpu.SemaphoreType.DMA((8,)),
            one, one, one, one, one, one,
        ],
        compiler_params=pltpu.CompilerParams(
            collective_id=0, has_side_effects=True, vmem_limit_bytes=60 << 20
        ),
        name="network_stack",
    )(jnp.transpose(fetch_list[0]), cluster_slots, moveouts, rec_flat, kernels,
      *masks(taps, width, used))
    return stack, peak.reshape(OUT)


def solution(mesh):
    placed = (
        P(("groups", "tmpl"), None, None),
        P("tmpl", None, None, None),
        P("tmpl", None, None),
        P("tmpl", None),
        P("tmpl", None),
    )
    return jax.shard_map(
        on_device,
        mesh=mesh,
        in_specs=placed,
        out_specs=(P(("groups", "tmpl"), None), P("groups")),
        check_vma=False,
    )
```

```python
import functools

import jax
import numpy as np
import jax.numpy as jnp
from jax import lax
from jax.experimental import pallas as pl
from jax.experimental.pallas import tpu as pltpu
from jax.sharding import PartitionSpec as P

OUT = 256
LANES = 128
FINE = 16
ROWS = OUT // FINE
PACK = LANES // FINE
SPLIT = 5


def push(src, dst, send, recv, peer):
    return pltpu.make_async_remote_copy(
        src_ref=src,
        dst_ref=dst,
        send_sem=send,
        recv_sem=recv,
        device_id={"tmpl": peer},
        device_id_type=pl.DeviceIdType.MESH,
    )


def each(low, high, action):
    if high - low == 1:
        action(low)
        return
    if low == 1 and high == 16:
        for d in (8, 9, 7, 10, 6, 11, 5, 12, 4, 13, 3, 14, 2, 15, 1):
            action(d)
        return

    def body(d, carry):
        action(d)
        return carry

    lax.fori_loop(low, high, body, 0)


def kernel(
    n, stations, sets, nstat, taps,
    list_hbm, slots_hbm, moves_hbm, rec_hbm, tm_hbm, band_hbm, shift_hbm, repeat_hbm,
    stack_ref, peak_ref,
    list_ref, slots_ref, moves_ref, rec_ref, tm_ref, req_ref, asked, want_ref, stage, rx_ref,
    hs, hl, tinv, weights, gains, turns, band, shift, repeat, windows, scales, first, xf, lines, mine, held,
    local, s1, r1, s2, r2, s3, r3,
):
    me = lax.axis_index("tmpl")
    tm_copy = pltpu.make_async_copy(tm_hbm, tm_ref, local.at[0])
    rec_copy = pltpu.make_async_copy(rec_hbm, rec_ref, local.at[1])
    list_copy = pltpu.make_async_copy(list_hbm, list_ref, local.at[2])
    slots_copy = pltpu.make_async_copy(slots_hbm, slots_ref, local.at[3])
    moves_copy = pltpu.make_async_copy(moves_hbm, moves_ref, local.at[4])
    list_copy.start()
    rec_copy.start()
    slots_copy.start()
    moves_copy.start()
    tm_copy.start()
    fixed = [
        pltpu.make_async_copy(band_hbm, band, local.at[5]),
        pltpu.make_async_copy(shift_hbm, shift, local.at[6]),
        pltpu.make_async_copy(repeat_hbm, repeat, local.at[7]),
    ]
    for copy in fixed:
        copy.start()

    barrier = pltpu.get_barrier_semaphore()
    each(1, n, lambda d: pl.semaphore_signal(
        barrier, inc=1, device_id={"tmpl": lax.rem(me + d, n)},
        device_id_type=pl.DeviceIdType.MESH))

    row = lax.broadcasted_iota(jnp.int32, (8, LANES), 0)
    lane = lax.broadcasted_iota(jnp.int32, (8, LANES), 1)
    pair = lax.broadcasted_iota(jnp.int32, (2, LANES), 0)

    def request(o):
        req_ref[o] = jnp.where(pair < 1, list_ref[0, o], list_ref[1, o])

    list_copy.wait()
    each(0, n, request)
    pl.semaphore_wait(barrier, n - 1)

    def ask(d):
        peer = lax.rem(me + d, n)
        return push(req_ref.at[peer], asked.at[d], s1, r1, peer)

    def give(d):
        peer = lax.rem(me + d, n)
        return push(stage.at[peer, pl.ds(0, 6)], rx_ref.at[d, pl.ds(0, 6)], s2, r2, peer)

    def tell(d):
        peer = lax.rem(me + d, n)
        return push(mine, held.at[d], s3, r3, peer)

    others = pl.ds(1, n - 1)

    def asks():
        return push(req_ref.at[others], asked.at[others], s1, r1, lax.rem(me + 1, n))

    def gives():
        six = pl.ds(0, 6)
        return push(stage.at[others, six], rx_ref.at[others, six], s2, r2, lax.rem(me + 1, n))

    def tells():
        return push(held.at[others], held.at[others], s3, r3, lax.rem(me + 1, n))

    each(1, n, lambda d: ask(d).start())
    asked[0] = req_ref[me]

    deep = hs.shape[1]
    pairs = sets * nstat
    lane16 = lax.broadcasted_iota(jnp.int32, (FINE, LANES), 1)
    row16 = lax.broadcasted_iota(jnp.int32, (FINE, LANES), 0)
    wide = windows.shape[0] // (6 * n) - 1
    tall = scales.shape[0] // (6 * n) - 1
    width = rec_ref.shape[1]

    def halves(x):
        high = x.astype(jnp.bfloat16)
        return high, (x - high.astype(jnp.float32)).astype(jnp.bfloat16)

    def series():
        for c in range(3):
            for k in range(sets):
                for v in range(deep):
                    end = min(taps - v * LANES, LANES)
                    some = tm_ref[k, c, :, v * LANES : v * LANES + end].astype(jnp.float32)
                    if end < LANES:
                        some = jnp.concatenate(
                            [some, jnp.zeros((nstat, LANES - end), jnp.float32)], axis=1)
                    hs[c, v, k * nstat : (k + 1) * nstat, :] = some
            power = jnp.concatenate([p for v in range(deep) for p in halves(hs[c, v] * hs[c, v])], axis=1)
            ones = jnp.ones((power.shape[1], LANES), jnp.bfloat16)
            total = jnp.dot(power, ones, preferred_element_type=jnp.float32)
            tinv[c] = 1.0 / (taps * jnp.sqrt(total / taps + 1e-05))
            head = lax.broadcasted_iota(jnp.int32, (pairs, LANES), 1) >= FINE
            moved = [
                pltpu.roll(hs[c, v].astype(jnp.bfloat16), FINE, 1).astype(jnp.float32) for v in range(deep)]
            for v in range(deep):
                hl[c, v] = jnp.where(head, moved[v], moved[v - 1] if v else 0.0)

    def prepare(at):
        fines = []
        for g in range(PACK):
            e = at * PACK + g
            k, j = e // nstat, lax.rem(e, nstat)
            slot, move = slots_ref[k, j], moves_ref[k, j]
            place = lax.rem(me - (slot >> 1) + n, n) * 6 + (slot & 1)
            first[0, e] = place * (wide + 1) + (move >> 4)
            first[1, e] = place * (tall + 1) + (move >> 4)
            fines.append(move & (FINE - 1))
        turn = jnp.zeros((8, LANES), jnp.int32)
        for g in range(PACK):
            turn = jnp.where(lane >= g * FINE, fines[g], turn)
        turns[at] = turn
        keep = lane16 >= row16
        for c in range(3):
            gain = jnp.zeros((8, LANES), jnp.float32)
            blocks = []
            for g in range(PACK):
                e = at * PACK + g
                turned = []
                for v in range(deep):
                    near = jnp.broadcast_to(hs[c, v, pl.ds(e, 1), :], (8, LANES))
                    far = jnp.broadcast_to(hl[c, v, pl.ds(e, 1), :], (8, LANES))
                    source = jnp.concatenate(
                        [jnp.where(row + i < fines[g], far, near) for i in range(0, FINE, 8)], axis=0)
                    turned.append(pltpu.roll(source.astype(jnp.bfloat16), 0, 1, stride=1, stride_axis=0))
                blocks.append([
                    jnp.where(keep, turned[v], turned[v - 1] if v else jnp.zeros_like(turned[0]))
                    for v in range(deep)])
                gain = jnp.where(
                    lane >= g * FINE, jnp.broadcast_to(tinv[c, pl.ds(e, 1), :], (8, LANES)), gain)
            gains[c, at] = gain
            for v in range(deep):
                weights[c, at, v * LANES : (v + 1) * LANES, :] = jnp.concatenate([b[v] for b in blocks], axis=0).T

    tm_copy.wait()
    slots_copy.wait()
    moves_copy.wait()
    series()
    each(0, SPLIT, prepare)
    rec_copy.wait()
    asks().wait_recv()
    rows = n * 8
    depth = rec_ref.shape[0]

    comp = row >> 1

    def spell(g):
        d = lax.rem(me - g + n, n)
        wanted = jnp.where((row & 1) == 0, asked[d, 0:1, :], asked[d, 1:2, :])
        valid = jnp.logical_and(wanted >= 0, row < 6)
        want_ref[g] = jnp.where(valid, comp * stations + wanted, -1)

    def gather(i):
        for g in range(16):
            spell(i * 16 + g)
        want = want_ref[pl.ds(i * 16, 16)].reshape(LANES, LANES)[:, :depth]
        spot = lax.broadcasted_iota(jnp.int32, (LANES, depth), 1)
        onehot = jnp.where(want == spot, 1.0, 0.0).astype(jnp.bfloat16)
        picked = jnp.dot(onehot, rec_ref[...], preferred_element_type=jnp.float32)
        stage[pl.ds(i * 16, 16)] = picked.reshape(16, 8, width).astype(jnp.bfloat16)

    each(0, n // 16, gather)
    each(1, n, lambda d: give(d).start())
    rx_ref[0] = stage[me]
    each(SPLIT, pairs // PACK, prepare)

    def unfold(i):
        size = 96
        for d in range(16):
            some = rx_ref[i * 16 + d].astype(jnp.float32)
            for v in range(width // LANES):
                xf[v, 6 * d : 6 * d + 6, :] = some[:6, v * LANES : (v + 1) * LANES]
        raw = jnp.concatenate([xf[v] for v in range(width // LANES)], axis=1)
        high, low = halves(raw * raw)
        samples = raw.astype(jnp.bfloat16)
        pieces = [samples[:, v * LANES : (v + 1) * LANES] for v in range(wide // 8)]
        pieces.append(jnp.zeros_like(pieces[0]))
        left = jnp.concatenate(
            [jnp.concatenate(pieces[v : v + 2], axis=1) for v in range(wide // 8)], axis=0)
        energy = jnp.dot(
            jnp.concatenate([high, low], axis=0), band[...], preferred_element_type=jnp.float32)
        out = jnp.dot(left, shift[...], preferred_element_type=jnp.float32)
        inverse = lax.rsqrt((energy[:size] + energy[size:]) / taps + 1e-05)
        high, low = halves(inverse)
        spread = jnp.concatenate(
            [jnp.concatenate([x[:, v * LANES : (v + 1) * LANES] for x in (high, low)], axis=1)
             for v in range(tall // 8)], axis=0)
        out2 = jnp.dot(spread, repeat[...], preferred_element_type=jnp.float32)
        base = i * size
        for target, value, count in ((windows, out, wide), (scales, out2, tall)):
            for v in range(count // 8):
                for x in range(PACK):
                    for q in range(0, size, 8):
                        target[pl.ds((base + q) * (count + 1) + 8 * v + x, 8, stride=count + 1), :] = (
                            value[v * size + q : v * size + q + 8, x * LANES : (x + 1) * LANES])

    def pick(parts):
        out = parts[0]
        for g in range(1, PACK):
            out = jnp.where(lane >= g * FINE, parts[g], out)
        return out

    def correlate(c, at):
        wraps = (lane & (FINE - 1)) < turns[at]
        starts = [[first[b, at * PACK + g] for g in range(PACK)] for b in range(2)]
        left = []
        for a in starts[0]:
            got = [windows[pl.ds(a + 2 * c * (wide + 1) + 8 * v, 8), :] for v in range(deep + 1)]
            left.append(jnp.concatenate(
                [jnp.concatenate(got[v : v + 2], axis=0) for v in range(deep)], axis=1))
        left = jnp.concatenate(left, axis=0).astype(jnp.bfloat16)
        got = lax.dot_general(
            left, weights[c, at], (((1,), (0,)), ((), ())), preferred_element_type=jnp.float32)
        gain = gains[c, at]
        for h in range(2):
            product = pick([got[FINE * g + 8 * h : FINE * g + 8 * h + 8] for g in range(PACK)])
            near = pick([scales[pl.ds(a + 2 * c * (tall + 1) + 8 * h, 8), :] for a in starts[1]])
            far = pick([scales[pl.ds(a + 2 * c * (tall + 1) + 8 * h + 1, 8), :] for a in starts[1]])
            term = product * (jnp.where(wraps, far, near) * gain)
            yield term

    for copy in fixed:
        copy.wait()
    gives().wait_recv()
    each(0, n // 16, unfold)
    sums = [[jnp.zeros((8, LANES), jnp.float32)] * 2 for _ in range(sets)]
    for at in range(pairs // PACK):
        order = (lane & (LANES - FINE)) + ((lane + turns[at]) & (FINE - 1))
        terms = [list(correlate(c, at)) for c in range(3)]
        for h in range(2):
            total = terms[0][h] + terms[1][h] + terms[2][h]
            out = jnp.take_along_axis(total, order, axis=1)
            for k in range(at * PACK // nstat, ((at + 1) * PACK - 1) // nstat + 1):
                low = max(k * nstat - at * PACK, 0)
                high = min((k + 1) * nstat - at * PACK, PACK)
                x = out
                if high - low < PACK:
                    x = jnp.where(jnp.logical_and(lane >= low * FINE, lane < high * FINE), x, 0.0)
                sums[k][h] = sums[k][h] + x
    for h in range(2):
        done = []
        for k in range(sets):
            x = sums[k][h]
            for size in (4 * FINE, 2 * FINE, FINE):
                x = x + pltpu.roll(x, size, 1)
            x = jnp.where((lane // FINE) == row, x, 0.0)
            done.append(jnp.sum(x, axis=0, keepdims=True))
        lines[h] = jnp.concatenate(done, axis=0)

    stack = jnp.concatenate([lines[0], lines[1]], axis=1)
    best = jnp.max(stack, axis=0, keepdims=True)
    mine[...] = best
    each(1, n, lambda d: tell(d).start())
    stack_ref[...] = stack
    held[0] = best
    tells().wait_recv()
    peak_ref[...] = jnp.max(held[...], axis=0)
    asks().wait_send()
    gives().wait_send()
    tells().wait_send()


def masks(taps, width, used):
    s, u = np.arange(width)[:, None], np.arange(used)[None]
    band = (s >= u) & (s < u + taps)
    s, u = np.arange(2 * LANES)[:, None], np.arange(PACK * LANES)[None]
    block, lane = u // LANES, u % LANES
    shift = s == lane + FINE * block
    repeat = s % LANES == lane % FINE + FINE * block
    return [jnp.asarray(x.astype(jnp.bfloat16)) for x in (band, shift, repeat)]


def on_device(records, templates, fetch_list, cluster_slots, moveouts):
    n = fetch_list.shape[1]
    stations, comps, width = records.shape
    sets, nstat = cluster_slots.shape
    taps = templates.shape[-1]
    deep = -(-(taps + 2 * FINE - 1) // LANES) * LANES
    most = width - OUT - taps + 1
    wide = -(-(most // FINE + ROWS + PACK * (deep // LANES - 1)) // 8) * 8
    tall = -(-(most // FINE + ROWS + 1) // 8) * 8
    used = -(-(OUT + most) // LANES) * LANES
    tiles = sets * nstat // PACK
    rec_flat = jnp.transpose(records, (1, 0, 2)).reshape(comps * stations, width)
    kernels = jnp.transpose(templates, (0, 2, 1, 3))
    vmem = pl.BlockSpec(memory_space=pltpu.VMEM)
    far = pl.BlockSpec(memory_space=pltpu.HBM)
    one = pltpu.SemaphoreType.DMA
    stack, peak = pl.pallas_call(
        functools.partial(kernel, n, stations, sets, nstat, taps),
        out_shape=(
            pltpu.VMEM((sets, OUT), jnp.float32),
            pltpu.VMEM((1, OUT), jnp.float32),
        ),
        in_specs=[far] * 8,
        out_specs=(vmem, vmem),
        scratch_shapes=[
            pltpu.SMEM((fetch_list.shape[2], n), jnp.int32),
            pltpu.SMEM(cluster_slots.shape, jnp.int32),
            pltpu.SMEM(moveouts.shape, jnp.int32),
            pltpu.VMEM(rec_flat.shape, jnp.bfloat16),
            pltpu.VMEM(kernels.shape, jnp.bfloat16),
            pltpu.VMEM((n, 2, LANES), jnp.int32),
            pltpu.VMEM((n, 2, LANES), jnp.int32),
            pltpu.VMEM((n, 8, LANES), jnp.int32),
            pltpu.VMEM((n, 8, width), jnp.bfloat16),
            pltpu.VMEM((n, 8, width), jnp.bfloat16),
            pltpu.VMEM((3, deep // LANES, sets * nstat, LANES), jnp.float32),
            pltpu.VMEM((3, deep // LANES, sets * nstat, LANES), jnp.float32),
            pltpu.VMEM((3, sets * nstat, LANES), jnp.float32),
            pltpu.VMEM((3, tiles, deep, LANES), jnp.bfloat16),
            pltpu.VMEM((3, tiles, 8, LANES), jnp.float32),
            pltpu.VMEM((tiles, 8, LANES), jnp.int32),
            pltpu.VMEM((width, used), jnp.bfloat16),
            pltpu.VMEM((2 * LANES, PACK * LANES), jnp.bfloat16),
            pltpu.VMEM((2 * LANES, PACK * LANES), jnp.bfloat16),
            pltpu.VMEM((n * 6 * (wide + 1), LANES), jnp.float32),
            pltpu.VMEM((n * 6 * (tall + 1), LANES), jnp.float32),
            pltpu.SMEM((2, sets * nstat), jnp.int32),
            pltpu.VMEM((width // LANES, 96, LANES), jnp.float32),
            pltpu.VMEM((2, sets, LANES), jnp.float32),
            pltpu.VMEM((1, OUT), jnp.float32),
            pltpu.VMEM((n, 1, OUT), jnp.float32),
            pltpu.SemaphoreType.DMA((8,)),
            one, one, one, one, one, one,
        ],
        compiler_params=pltpu.CompilerParams(
            collective_id=0, has_side_effects=True, vmem_limit_bytes=60 << 20
        ),
        name="network_stack",
    )(jnp.transpose(fetch_list[0]), cluster_slots, moveouts, rec_flat, kernels,
      *masks(taps, width, used))
    return stack, peak.reshape(OUT)


def solution(mesh):
    placed = (
        P(("groups", "tmpl"), None, None),
        P("tmpl", None, None, None),
        P("tmpl", None, None),
        P("tmpl", None),
        P("tmpl", None),
    )
    return jax.shard_map(
        on_device,
        mesh=mesh,
        in_specs=placed,
        out_specs=(P(("groups", "tmpl"), None), P("groups")),
        check_vma=False,
    )
```

```python
import functools

import jax
import numpy as np
import jax.numpy as jnp
from jax import lax
from jax.experimental import pallas as pl
from jax.experimental.pallas import tpu as pltpu
from jax.sharding import PartitionSpec as P

OUT = 256
LANES = 128
FINE = 16
ROWS = OUT // FINE
PACK = LANES // FINE
SPLIT = 5


def push(src, dst, send, recv, peer):
    return pltpu.make_async_remote_copy(
        src_ref=src,
        dst_ref=dst,
        send_sem=send,
        recv_sem=recv,
        device_id={"tmpl": peer},
        device_id_type=pl.DeviceIdType.MESH,
    )


def each(low, high, action):
    if high - low == 1:
        action(low)
        return
    if low == 1 and high == 16:
        for d in (8, 9, 7, 10, 6, 11, 5, 12, 4, 13, 3, 14, 2, 15, 1):
            action(d)
        return

    def body(d, carry):
        action(d)
        return carry

    lax.fori_loop(low, high, body, 0)


def kernel(
    n, stations, sets, nstat, taps,
    list_hbm, slots_hbm, moves_hbm, rec_hbm, tm_hbm, band_hbm, shift_hbm, repeat_hbm,
    stack_ref, peak_ref,
    list_ref, slots_ref, moves_ref, rec_ref, tm_ref, req_ref, asked, want_ref, stage, rx_ref,
    hs, hl, tinv, weights, gains, turns, band, shift, repeat, windows, scales, first, xf, lines, mine, held,
    local, s1, r1, s2, r2, s3, r3,
):
    me = lax.axis_index("tmpl")
    tm_copy = pltpu.make_async_copy(tm_hbm, tm_ref, local.at[0])
    rec_copy = pltpu.make_async_copy(rec_hbm, rec_ref, local.at[1])
    list_copy = pltpu.make_async_copy(list_hbm, list_ref, local.at[2])
    slots_copy = pltpu.make_async_copy(slots_hbm, slots_ref, local.at[3])
    moves_copy = pltpu.make_async_copy(moves_hbm, moves_ref, local.at[4])
    list_copy.start()
    rec_copy.start()
    slots_copy.start()
    moves_copy.start()
    tm_copy.start()
    fixed = [
        pltpu.make_async_copy(band_hbm, band, local.at[5]),
        pltpu.make_async_copy(shift_hbm, shift, local.at[6]),
        pltpu.make_async_copy(repeat_hbm, repeat, local.at[7]),
    ]
    for copy in fixed:
        copy.start()

    barrier = pltpu.get_barrier_semaphore()
    each(1, n, lambda d: pl.semaphore_signal(
        barrier, inc=1, device_id={"tmpl": lax.rem(me + d, n)},
        device_id_type=pl.DeviceIdType.MESH))

    row = lax.broadcasted_iota(jnp.int32, (8, LANES), 0)
    lane = lax.broadcasted_iota(jnp.int32, (8, LANES), 1)
    pair = lax.broadcasted_iota(jnp.int32, (2, LANES), 0)

    def request(o):
        req_ref[o] = jnp.where(pair < 1, list_ref[0, o], list_ref[1, o])

    list_copy.wait()
    each(0, n, request)
    pl.semaphore_wait(barrier, n - 1)

    def ask(d):
        peer = lax.rem(me + d, n)
        return push(req_ref.at[peer], asked.at[d], s1, r1, peer)

    def give(d):
        peer = lax.rem(me + d, n)
        return push(stage.at[d, pl.ds(0, 6)], rx_ref.at[d, pl.ds(0, 6)], s2, r2, peer)

    def tell(d):
        peer = lax.rem(me + d, n)
        return push(mine, held.at[d], s3, r3, peer)

    others = pl.ds(1, n - 1)

    def asks():
        return push(req_ref.at[others], asked.at[others], s1, r1, lax.rem(me + 1, n))

    def gives():
        six = pl.ds(0, 6)
        return push(stage.at[others, six], rx_ref.at[others, six], s2, r2, lax.rem(me + 1, n))

    def tells():
        return push(held.at[others], held.at[others], s3, r3, lax.rem(me + 1, n))

    each(1, n, lambda d: ask(d).start())
    asked[0] = req_ref[me]

    deep = hs.shape[1]
    pairs = sets * nstat
    lane16 = lax.broadcasted_iota(jnp.int32, (FINE, LANES), 1)
    row16 = lax.broadcasted_iota(jnp.int32, (FINE, LANES), 0)
    wide = windows.shape[0] // (6 * n) - 1
    tall = scales.shape[0] // (6 * n) - 1
    width = rec_ref.shape[1]

    def halves(x):
        high = x.astype(jnp.bfloat16)
        return high, (x - high.astype(jnp.float32)).astype(jnp.bfloat16)

    def series():
        for c in range(3):
            for k in range(sets):
                for v in range(deep):
                    end = min(taps - v * LANES, LANES)
                    some = tm_ref[k, c, :, v * LANES : v * LANES + end].astype(jnp.float32)
                    if end < LANES:
                        some = jnp.concatenate(
                            [some, jnp.zeros((nstat, LANES - end), jnp.float32)], axis=1)
                    hs[c, v, k * nstat : (k + 1) * nstat, :] = some
            power = jnp.concatenate([p for v in range(deep) for p in halves(hs[c, v] * hs[c, v])], axis=1)
            ones = jnp.ones((power.shape[1], LANES), jnp.bfloat16)
            total = jnp.dot(power, ones, preferred_element_type=jnp.float32)
            tinv[c] = 1.0 / (taps * jnp.sqrt(total / taps + 1e-05))
            head = lax.broadcasted_iota(jnp.int32, (pairs, LANES), 1) >= FINE
            moved = [
                pltpu.roll(hs[c, v].astype(jnp.bfloat16), FINE, 1).astype(jnp.float32) for v in range(deep)]
            for v in range(deep):
                hl[c, v] = jnp.where(head, moved[v], moved[v - 1] if v else 0.0)

    def prepare(at):
        fines = []
        for g in range(PACK):
            e = at * PACK + g
            k, j = e // nstat, lax.rem(e, nstat)
            slot, move = slots_ref[k, j], moves_ref[k, j]
            place = lax.rem(me - (slot >> 1) + n, n) * 6 + (slot & 1)
            first[0, e] = place * (wide + 1) + (move >> 4)
            first[1, e] = place * (tall + 1) + (move >> 4)
            fines.append(move & (FINE - 1))
        turn = jnp.zeros((8, LANES), jnp.int32)
        for g in range(PACK):
            turn = jnp.where(lane >= g * FINE, fines[g], turn)
        turns[at] = turn
        keep = lane16 >= row16
        for c in range(3):
            gain = jnp.zeros((8, LANES), jnp.float32)
            blocks = []
            for g in range(PACK):
                e = at * PACK + g
                turned = []
                for v in range(deep):
                    near = jnp.broadcast_to(hs[c, v, pl.ds(e, 1), :], (8, LANES))
                    far = jnp.broadcast_to(hl[c, v, pl.ds(e, 1), :], (8, LANES))
                    source = jnp.concatenate(
                        [jnp.where(row + i < fines[g], far, near) for i in range(0, FINE, 8)], axis=0)
                    turned.append(pltpu.roll(source.astype(jnp.bfloat16), 0, 1, stride=1, stride_axis=0))
                blocks.append([
                    jnp.where(keep, turned[v], turned[v - 1] if v else jnp.zeros_like(turned[0]))
                    for v in range(deep)])
                gain = jnp.where(
                    lane >= g * FINE, jnp.broadcast_to(tinv[c, pl.ds(e, 1), :], (8, LANES)), gain)
            gains[c, at] = gain
            for v in range(deep):
                weights[c, at, v * LANES : (v + 1) * LANES, :] = jnp.concatenate([b[v] for b in blocks], axis=0).T

    tm_copy.wait()
    slots_copy.wait()
    moves_copy.wait()
    series()
    each(0, SPLIT, prepare)
    rec_copy.wait()
    asks().wait_recv()
    rows = n * 8
    depth = rec_ref.shape[0]

    comp = row >> 1

    def spell(d):
        at = (n - d) % n if isinstance(d, int) else lax.rem(n - d, n)
        wanted = jnp.where((row & 1) == 0, asked[at, 0:1, :], asked[at, 1:2, :])
        valid = jnp.logical_and(wanted >= 0, row < 6)
        want_ref[d] = jnp.where(valid, comp * stations + wanted, -1)

    def gather(i):
        for d in range(8):
            spell(i * 8 + d)
        want = want_ref[pl.ds(i * 8, 8)].reshape(64, LANES)[:, :depth]
        spot = lax.broadcasted_iota(jnp.int32, (64, depth), 1)
        onehot = jnp.where(want == spot, 1.0, 0.0).astype(jnp.bfloat16)
        picked = jnp.dot(onehot, rec_ref[...], preferred_element_type=jnp.float32)
        stage[pl.ds(i * 8, 8)] = picked.reshape(8, 8, width).astype(jnp.bfloat16)

    each(1, n // 8, gather)
    gather(0)
    each(1, n, lambda d: give(d).start())
    rx_ref[0] = stage[0]
    each(SPLIT, pairs // PACK, prepare)

    used = band.shape[1]

    def unfold(i):
        size = 96
        for d in range(16):
            some = rx_ref[i * 16 + d].astype(jnp.float32)
            for v in range(width // LANES):
                xf[v, 6 * d : 6 * d + 6, :] = some[:6, v * LANES : (v + 1) * LANES]
        raw = jnp.concatenate([xf[v] for v in range(width // LANES)], axis=1)
        high, low = halves(raw * raw)
        samples = raw.astype(jnp.bfloat16)
        pieces = [samples[:, v * LANES : (v + 1) * LANES] for v in range(wide // 8)]
        pieces.append(jnp.zeros_like(pieces[0]))
        left = jnp.concatenate(
            [jnp.concatenate(pieces[v : v + 2], axis=1) for v in range(wide // 8)], axis=0)
        both = jnp.concatenate([high, low], axis=0)
        half = 2 * LANES
        reach = -(-(half + taps - 1) // half) * half
        energy = jnp.concatenate([
            jnp.dot(both[:, at : at + reach], band[at : at + reach, at : at + half], preferred_element_type=jnp.float32)
            for at in range(0, used, half)], axis=1)
        out = jnp.dot(left, shift[...], preferred_element_type=jnp.float32)
        inverse = lax.rsqrt((energy[:size] + energy[size:]) / taps + 1e-05)
        high, low = halves(inverse)
        spread = jnp.concatenate(
            [jnp.concatenate([x[:, v * LANES : (v + 1) * LANES] for x in (high, low)], axis=1)
             for v in range(tall // 8)], axis=0)
        out2 = jnp.dot(spread, repeat[...], preferred_element_type=jnp.float32)
        base = i * size
        for target, value, count in ((windows, out, wide), (scales, out2, tall)):
            for v in range(count // 8):
                for x in range(PACK):
                    for q in range(0, size, 8):
                        target[pl.ds((base + q) * (count + 1) + 8 * v + x, 8, stride=count + 1), :] = (
                            value[v * size + q : v * size + q + 8, x * LANES : (x + 1) * LANES])

    def pick(parts):
        out = parts[0]
        for g in range(1, PACK):
            out = jnp.where(lane >= g * FINE, parts[g], out)
        return out

    def correlate(c, at):
        wraps = (lane & (FINE - 1)) < turns[at]
        starts = [[first[b, at * PACK + g] for g in range(PACK)] for b in range(2)]
        left = []
        for a in starts[0]:
            got = [windows[pl.ds(a + 2 * c * (wide + 1) + 8 * v, 8), :] for v in range(deep + 1)]
            left.append(jnp.concatenate(
                [jnp.concatenate(got[v : v + 2], axis=0) for v in range(deep)], axis=1))
        left = jnp.concatenate(left, axis=0).astype(jnp.bfloat16)
        got = lax.dot_general(
            left, weights[c, at], (((1,), (0,)), ((), ())), preferred_element_type=jnp.float32)
        gain = gains[c, at]
        for h in range(2):
            product = pick([got[FINE * g + 8 * h : FINE * g + 8 * h + 8] for g in range(PACK)])
            near = pick([scales[pl.ds(a + 2 * c * (tall + 1) + 8 * h, 8), :] for a in starts[1]])
            far = pick([scales[pl.ds(a + 2 * c * (tall + 1) + 8 * h + 1, 8), :] for a in starts[1]])
            term = product * (jnp.where(wraps, far, near) * gain)
            yield term

    for copy in fixed:
        copy.wait()
    gives().wait_recv()
    each(0, n // 16, unfold)
    sums = [[jnp.zeros((8, LANES), jnp.float32)] * 2 for _ in range(sets)]
    for at in range(pairs // PACK):
        order = (lane & (LANES - FINE)) + ((lane + turns[at]) & (FINE - 1))
        terms = [list(correlate(c, at)) for c in range(3)]
        for h in range(2):
            total = terms[0][h] + terms[1][h] + terms[2][h]
            out = jnp.take_along_axis(total, order, axis=1)
            for k in range(at * PACK // nstat, ((at + 1) * PACK - 1) // nstat + 1):
                low = max(k * nstat - at * PACK, 0)
                high = min((k + 1) * nstat - at * PACK, PACK)
                x = out
                if high - low < PACK:
                    x = jnp.where(jnp.logical_and(lane >= low * FINE, lane < high * FINE), x, 0.0)
                sums[k][h] = sums[k][h] + x
    for h in range(2):
        done = []
        for k in range(sets):
            x = sums[k][h]
            for size in (4 * FINE, 2 * FINE, FINE):
                x = x + pltpu.roll(x, size, 1)
            x = jnp.where((lane // FINE) == row, x, 0.0)
            done.append(jnp.sum(x, axis=0, keepdims=True))
        lines[h] = jnp.concatenate(done, axis=0)

    stack = jnp.concatenate([lines[0], lines[1]], axis=1)
    best = jnp.max(stack, axis=0, keepdims=True)
    mine[...] = best
    each(1, n, lambda d: tell(d).start())
    stack_ref[...] = stack
    held[0] = best
    tells().wait_recv()
    peak_ref[...] = jnp.max(held[...], axis=0)
    asks().wait_send()
    gives().wait_send()
    tells().wait_send()


def hand_out(stack_in, peak_in, stack_out, peak_out, sems):
    copies = [
        pltpu.make_async_copy(stack_in, stack_out, sems.at[0]),
        pltpu.make_async_copy(peak_in, peak_out, sems.at[1]),
    ]
    for copy in copies:
        copy.start()
    for copy in copies:
        copy.wait()


def masks(taps, width, used):
    s, u = np.arange(width)[:, None], np.arange(used)[None]
    band = (s >= u) & (s < u + taps)
    s, u = np.arange(2 * LANES)[:, None], np.arange(PACK * LANES)[None]
    block, lane = u // LANES, u % LANES
    shift = s == lane + FINE * block
    repeat = s % LANES == lane % FINE + FINE * block
    return [jnp.asarray(x.astype(jnp.bfloat16)) for x in (band, shift, repeat)]


def on_device(records, templates, fetch_list, cluster_slots, moveouts):
    n = fetch_list.shape[1]
    stations, comps, width = records.shape
    sets, nstat = cluster_slots.shape
    taps = templates.shape[-1]
    deep = -(-(taps + 2 * FINE - 1) // LANES) * LANES
    most = width - OUT - taps + 1
    wide = -(-(most // FINE + ROWS + PACK * (deep // LANES - 1)) // 8) * 8
    tall = -(-(most // FINE + ROWS + 1) // 8) * 8
    used = -(-(OUT + most) // LANES) * LANES
    tiles = sets * nstat // PACK
    rec_flat = jnp.transpose(records, (1, 0, 2)).reshape(comps * stations, width)
    kernels = jnp.transpose(templates, (0, 2, 1, 3))
    vmem = pl.BlockSpec(memory_space=pltpu.VMEM)
    far = pl.BlockSpec(memory_space=pltpu.HBM)
    one = pltpu.SemaphoreType.DMA
    stack, peak = pl.pallas_call(
        functools.partial(kernel, n, stations, sets, nstat, taps),
        out_shape=(
            pltpu.VMEM((sets, OUT), jnp.float32),
            pltpu.VMEM((1, OUT), jnp.float32),
        ),
        in_specs=[far] * 8,
        out_specs=(vmem, vmem),
        scratch_shapes=[
            pltpu.SMEM((fetch_list.shape[2], n), jnp.int32),
            pltpu.SMEM(cluster_slots.shape, jnp.int32),
            pltpu.SMEM(moveouts.shape, jnp.int32),
            pltpu.VMEM(rec_flat.shape, jnp.bfloat16),
            pltpu.VMEM(kernels.shape, jnp.bfloat16),
            pltpu.VMEM((n, 2, LANES), jnp.int32),
            pltpu.VMEM((n, 2, LANES), jnp.int32),
            pltpu.VMEM((n, 8, LANES), jnp.int32),
            pltpu.VMEM((n, 8, width), jnp.bfloat16),
            pltpu.VMEM((n, 8, width), jnp.bfloat16),
            pltpu.VMEM((3, deep // LANES, sets * nstat, LANES), jnp.float32),
            pltpu.VMEM((3, deep // LANES, sets * nstat, LANES), jnp.float32),
            pltpu.VMEM((3, sets * nstat, LANES), jnp.float32),
            pltpu.VMEM((3, tiles, deep, LANES), jnp.bfloat16),
            pltpu.VMEM((3, tiles, 8, LANES), jnp.float32),
            pltpu.VMEM((tiles, 8, LANES), jnp.int32),
            pltpu.VMEM((width, used), jnp.bfloat16),
            pltpu.VMEM((2 * LANES, PACK * LANES), jnp.bfloat16),
            pltpu.VMEM((2 * LANES, PACK * LANES), jnp.bfloat16),
            pltpu.VMEM((n * 6 * (wide + 1), LANES), jnp.float32),
            pltpu.VMEM((n * 6 * (tall + 1), LANES), jnp.float32),
            pltpu.SMEM((2, sets * nstat), jnp.int32),
            pltpu.VMEM((width // LANES, 96, LANES), jnp.float32),
            pltpu.VMEM((2, sets, LANES), jnp.float32),
            pltpu.VMEM((1, OUT), jnp.float32),
            pltpu.VMEM((n, 1, OUT), jnp.float32),
            pltpu.SemaphoreType.DMA((8,)),
            one, one, one, one, one, one,
        ],
        compiler_params=pltpu.CompilerParams(
            collective_id=0, has_side_effects=True, vmem_limit_bytes=60 << 20
        ),
        name="network_stack",
    )(jnp.transpose(fetch_list[0]), cluster_slots, moveouts, rec_flat, kernels,
      *masks(taps, width, used))
    anywhere = pl.BlockSpec(memory_space=pl.ANY)
    stack, peak = pl.pallas_call(
        hand_out,
        out_shape=(
            jax.ShapeDtypeStruct((sets, OUT), jnp.float32),
            jax.ShapeDtypeStruct((1, OUT), jnp.float32),
        ),
        in_specs=[vmem] * 2,
        out_specs=[anywhere] * 2,
        scratch_shapes=[pltpu.SemaphoreType.DMA((2,))],
        name="hand_out",
    )(*[pltpu.with_memory_space_constraint(x, pltpu.VMEM) for x in (stack, peak)])
    return stack, peak.reshape(OUT)


def solution(mesh):
    placed = (
        P(("groups", "tmpl"), None, None),
        P("tmpl", None, None, None),
        P("tmpl", None, None),
        P("tmpl", None),
        P("tmpl", None),
    )
    return jax.shard_map(
        on_device,
        mesh=mesh,
        in_specs=placed,
        out_specs=(P(("groups", "tmpl"), None), P("groups")),
        check_vma=False,
    )
```

```python
import functools

import jax
import numpy as np
import jax.numpy as jnp
from jax import lax
from jax.experimental import pallas as pl
from jax.experimental.pallas import tpu as pltpu
from jax.sharding import PartitionSpec as P

OUT = 256
LANES = 128
FINE = 16
ROWS = OUT // FINE
PACK = LANES // FINE
SPLIT = 5


def push(src, dst, send, recv, peer):
    return pltpu.make_async_remote_copy(
        src_ref=src,
        dst_ref=dst,
        send_sem=send,
        recv_sem=recv,
        device_id={"tmpl": peer},
        device_id_type=pl.DeviceIdType.MESH,
    )


def each(low, high, action):
    if high - low == 1:
        action(low)
        return
    if low == 1 and high == 16:
        for d in (8, 9, 7, 10, 6, 11, 5, 12, 4, 13, 3, 14, 2, 15, 1):
            action(d)
        return

    def body(d, carry):
        action(d)
        return carry

    lax.fori_loop(low, high, body, 0)


def kernel(
    n, stations, sets, nstat, taps,
    list_hbm, slots_hbm, moves_hbm, rec_hbm, tm_hbm, band_hbm, shift_hbm, repeat_hbm,
    stack_ref, peak_ref,
    list_ref, slots_ref, moves_ref, rec_ref, tm_ref, req_ref, asked, want_ref, stage, rx_ref,
    hs, hl, tinv, weights, gains, turns, band, shift, repeat, windows, scales, first, xf, lines, mine, held,
    local, s1, r1, s2, r2, s3, r3,
):
    me = lax.axis_index("tmpl")
    tm_copy = pltpu.make_async_copy(tm_hbm, tm_ref, local.at[0])
    rec_copy = pltpu.make_async_copy(rec_hbm, rec_ref, local.at[1])
    list_copy = pltpu.make_async_copy(list_hbm, list_ref, local.at[2])
    slots_copy = pltpu.make_async_copy(slots_hbm, slots_ref, local.at[3])
    moves_copy = pltpu.make_async_copy(moves_hbm, moves_ref, local.at[4])
    list_copy.start()
    rec_copy.start()
    slots_copy.start()
    moves_copy.start()
    tm_copy.start()
    fixed = [
        pltpu.make_async_copy(band_hbm, band, local.at[5]),
        pltpu.make_async_copy(shift_hbm, shift, local.at[6]),
        pltpu.make_async_copy(repeat_hbm, repeat, local.at[7]),
    ]
    for copy in fixed:
        copy.start()

    barrier = pltpu.get_barrier_semaphore()
    each(1, n, lambda d: pl.semaphore_signal(
        barrier, inc=1, device_id={"tmpl": lax.rem(me + d, n)},
        device_id_type=pl.DeviceIdType.MESH))

    row = lax.broadcasted_iota(jnp.int32, (8, LANES), 0)
    lane = lax.broadcasted_iota(jnp.int32, (8, LANES), 1)
    pair = lax.broadcasted_iota(jnp.int32, (2, LANES), 0)

    def request(o):
        req_ref[o] = jnp.where(pair < 1, list_ref[0, o], list_ref[1, o])

    list_copy.wait()
    each(0, n, request)
    pl.semaphore_wait(barrier, n - 1)

    def ask(d):
        peer = lax.rem(me + d, n)
        return push(req_ref.at[peer], asked.at[d], s1, r1, peer)

    def give(d):
        peer = lax.rem(me + d, n)
        return push(stage.at[d, pl.ds(0, 6)], rx_ref.at[d, pl.ds(0, 6)], s2, r2, peer)

    def tell(d):
        peer = lax.rem(me + d, n)
        return push(mine, held.at[d], s3, r3, peer)

    others = pl.ds(1, n - 1)

    def asks():
        return push(req_ref.at[others], asked.at[others], s1, r1, lax.rem(me + 1, n))

    def gives():
        six = pl.ds(0, 6)
        return push(stage.at[others, six], rx_ref.at[others, six], s2, r2, lax.rem(me + 1, n))

    def tells():
        return push(held.at[others], held.at[others], s3, r3, lax.rem(me + 1, n))

    each(1, n, lambda d: ask(d).start())
    asked[0] = req_ref[me]

    deep = hs.shape[1]
    pairs = sets * nstat
    lane16 = lax.broadcasted_iota(jnp.int32, (FINE, LANES), 1)
    row16 = lax.broadcasted_iota(jnp.int32, (FINE, LANES), 0)
    wide = windows.shape[0] // (6 * n) - 1
    tall = scales.shape[0] // (6 * n) - 1
    width = rec_ref.shape[1]

    def halves(x):
        high = x.astype(jnp.bfloat16)
        return high, (x - high.astype(jnp.float32)).astype(jnp.bfloat16)

    def series():
        for c in range(3):
            for k in range(sets):
                for v in range(deep):
                    end = min(taps - v * LANES, LANES)
                    some = tm_ref[k, c, :, v * LANES : v * LANES + end].astype(jnp.float32)
                    if end < LANES:
                        some = jnp.concatenate(
                            [some, jnp.zeros((nstat, LANES - end), jnp.float32)], axis=1)
                    hs[c, v, k * nstat : (k + 1) * nstat, :] = some
            power = jnp.concatenate([p for v in range(deep) for p in halves(hs[c, v] * hs[c, v])], axis=1)
            ones = jnp.ones((power.shape[1], LANES), jnp.bfloat16)
            total = jnp.dot(power, ones, preferred_element_type=jnp.float32)
            tinv[c] = 1.0 / (taps * jnp.sqrt(total / taps + 1e-05))
            head = lax.broadcasted_iota(jnp.int32, (pairs, LANES), 1) >= FINE
            moved = [
                pltpu.roll(hs[c, v].astype(jnp.bfloat16), FINE, 1).astype(jnp.float32) for v in range(deep)]
            for v in range(deep):
                hl[c, v] = jnp.where(head, moved[v], moved[v - 1] if v else 0.0)

    def prepare(at):
        fines = []
        for g in range(PACK):
            e = at * PACK + g
            k, j = e // nstat, lax.rem(e, nstat)
            slot, move = slots_ref[k, j], moves_ref[k, j]
            place = lax.rem(me - (slot >> 1) + n, n) * 6 + (slot & 1)
            first[0, e] = place * (wide + 1) + (move >> 4)
            first[1, e] = place * (tall + 1) + (move >> 4)
            fines.append(move & (FINE - 1))
        turn = jnp.zeros((8, LANES), jnp.int32)
        for g in range(PACK):
            turn = jnp.where(lane >= g * FINE, fines[g], turn)
        turns[at] = turn
        keep = lane16 >= row16
        for c in range(3):
            gain = jnp.zeros((8, LANES), jnp.float32)
            blocks = []
            for g in range(PACK):
                e = at * PACK + g
                turned = []
                for v in range(deep):
                    near = jnp.broadcast_to(hs[c, v, pl.ds(e, 1), :], (8, LANES))
                    far = jnp.broadcast_to(hl[c, v, pl.ds(e, 1), :], (8, LANES))
                    source = jnp.concatenate(
                        [jnp.where(row + i < fines[g], far, near) for i in range(0, FINE, 8)], axis=0)
                    turned.append(pltpu.roll(source.astype(jnp.bfloat16), 0, 1, stride=1, stride_axis=0))
                blocks.append([
                    jnp.where(keep, turned[v], turned[v - 1] if v else jnp.zeros_like(turned[0]))
                    for v in range(deep)])
                gain = jnp.where(
                    lane >= g * FINE, jnp.broadcast_to(tinv[c, pl.ds(e, 1), :], (8, LANES)), gain)
            gains[c, at] = gain
            for v in range(deep):
                weights[c, at, v * LANES : (v + 1) * LANES, :] = jnp.concatenate([b[v] for b in blocks], axis=0).T

    tm_copy.wait()
    slots_copy.wait()
    moves_copy.wait()
    series()
    each(0, SPLIT, prepare)
    rec_copy.wait()
    asks().wait_recv()
    rows = n * 8
    depth = rec_ref.shape[0]

    comp = row >> 1

    def spell(d):
        at = (n - d) % n if isinstance(d, int) else lax.rem(n - d, n)
        wanted = jnp.where((row & 1) == 0, asked[at, 0:1, :], asked[at, 1:2, :])
        valid = jnp.logical_and(wanted >= 0, row < 6)
        want_ref[d] = jnp.where(valid, comp * stations + wanted, -1)

    def gather(i):
        for d in range(8):
            spell(i * 8 + d)
        want = want_ref[pl.ds(i * 8, 8)].reshape(64, LANES)[:, :depth]
        spot = lax.broadcasted_iota(jnp.int32, (64, depth), 1)
        onehot = jnp.where(want == spot, 1.0, 0.0).astype(jnp.bfloat16)
        picked = jnp.dot(onehot, rec_ref[...], preferred_element_type=jnp.float32)
        stage[pl.ds(i * 8, 8)] = picked.reshape(8, 8, width).astype(jnp.bfloat16)

    each(1, n // 8, gather)
    gather(0)
    each(1, n, lambda d: give(d).start())
    rx_ref[0] = stage[0]
    each(SPLIT, pairs // PACK, prepare)

    used = band.shape[1]

    def unfold(i):
        size = 96
        for d in range(16):
            some = rx_ref[i * 16 + d].astype(jnp.float32)
            for v in range(width // LANES):
                xf[v, 6 * d : 6 * d + 6, :] = some[:6, v * LANES : (v + 1) * LANES]
        raw = jnp.concatenate([xf[v] for v in range(width // LANES)], axis=1)
        high, low = halves(raw * raw)
        samples = raw.astype(jnp.bfloat16)
        pieces = [samples[:, v * LANES : (v + 1) * LANES] for v in range(wide // 8)]
        pieces.append(jnp.zeros_like(pieces[0]))
        left = jnp.concatenate(
            [jnp.concatenate(pieces[v : v + 2], axis=1) for v in range(wide // 8)], axis=0)
        both = jnp.concatenate([high, low], axis=0)
        half = 2 * LANES
        reach = -(-(half + taps - 1) // half) * half
        energy = jnp.concatenate([
            jnp.dot(both[:, at : at + reach], band[at : at + reach, at : at + half], preferred_element_type=jnp.float32)
            for at in range(0, used, half)], axis=1)
        out = jnp.dot(left, shift[...], preferred_element_type=jnp.float32)
        inverse = lax.rsqrt((energy[:size] + energy[size:]) / taps + 1e-05)
        high, low = halves(inverse)
        spread = jnp.concatenate(
            [jnp.concatenate([x[:, v * LANES : (v + 1) * LANES] for x in (high, low)], axis=1)
             for v in range(tall // 8)], axis=0)
        out2 = jnp.dot(spread, repeat[...], preferred_element_type=jnp.float32)
        base = i * size
        for target, value, count in ((windows, out, wide), (scales, out2, tall)):
            for v in range(count // 8):
                for x in range(PACK):
                    for q in range(0, size, 8):
                        target[pl.ds((base + q) * (count + 1) + 8 * v + x, 8, stride=count + 1), :] = (
                            value[v * size + q : v * size + q + 8, x * LANES : (x + 1) * LANES])

    def pick(parts):
        out = parts[0]
        for g in range(1, PACK):
            out = jnp.where(lane >= g * FINE, parts[g], out)
        return out

    def correlate(c, at):
        wraps = (lane & (FINE - 1)) < turns[at]
        starts = [[first[b, at * PACK + g] for g in range(PACK)] for b in range(2)]
        left = []
        for a in starts[0]:
            got = [windows[pl.ds(a + 2 * c * (wide + 1) + 8 * v, 8), :] for v in range(deep + 1)]
            left.append(jnp.concatenate(
                [jnp.concatenate(got[v : v + 2], axis=0) for v in range(deep)], axis=1))
        left = jnp.concatenate(left, axis=0).astype(jnp.bfloat16)
        got = lax.dot_general(
            left, weights[c, at], (((1,), (0,)), ((), ())), preferred_element_type=jnp.float32)
        gain = gains[c, at]
        for h in range(2):
            product = pick([got[FINE * g + 8 * h : FINE * g + 8 * h + 8] for g in range(PACK)])
            near = pick([scales[pl.ds(a + 2 * c * (tall + 1) + 8 * h, 8), :] for a in starts[1]])
            far = pick([scales[pl.ds(a + 2 * c * (tall + 1) + 8 * h + 1, 8), :] for a in starts[1]])
            term = product * (jnp.where(wraps, far, near) * gain)
            yield term

    for copy in fixed:
        copy.wait()
    gives().wait_recv()
    each(0, n // 16, unfold)
    sums = [[jnp.zeros((8, LANES), jnp.float32)] * 2 for _ in range(sets)]
    for at in range(pairs // PACK):
        order = (lane & (LANES - FINE)) + ((lane + turns[at]) & (FINE - 1))
        terms = [list(correlate(c, at)) for c in range(3)]
        for h in range(2):
            total = terms[0][h] + terms[1][h] + terms[2][h]
            out = jnp.take_along_axis(total, order, axis=1)
            for k in range(at * PACK // nstat, ((at + 1) * PACK - 1) // nstat + 1):
                low = max(k * nstat - at * PACK, 0)
                high = min((k + 1) * nstat - at * PACK, PACK)
                x = out
                if high - low < PACK:
                    x = jnp.where(jnp.logical_and(lane >= low * FINE, lane < high * FINE), x, 0.0)
                sums[k][h] = sums[k][h] + x
    for h in range(2):
        done = []
        for k in range(sets):
            x = sums[k][h]
            for size in (4 * FINE, 2 * FINE, FINE):
                x = x + pltpu.roll(x, size, 1)
            x = jnp.where((lane // FINE) == row, x, 0.0)
            done.append(jnp.sum(x, axis=0, keepdims=True))
        lines[h] = jnp.concatenate(done, axis=0)

    stack = jnp.concatenate([lines[0], lines[1]], axis=1)
    best = jnp.max(stack, axis=0, keepdims=True)
    mine[...] = best
    each(1, n, lambda d: tell(d).start())
    stack_ref[...] = stack
    held[0] = best
    asks().wait_send()
    gives().wait_send()
    tells().wait_recv()
    peak_ref[...] = jnp.max(held[...], axis=0)
    tells().wait_send()


def hand_out(stack_in, peak_in, stack_out, peak_out, sems):
    copies = [
        pltpu.make_async_copy(stack_in, stack_out, sems.at[0]),
        pltpu.make_async_copy(peak_in, peak_out, sems.at[1]),
    ]
    for copy in copies:
        copy.start()
    for copy in copies:
        copy.wait()


def masks(taps, width, used):
    s, u = np.arange(width)[:, None], np.arange(used)[None]
    band = (s >= u) & (s < u + taps)
    s, u = np.arange(2 * LANES)[:, None], np.arange(PACK * LANES)[None]
    block, lane = u // LANES, u % LANES
    shift = s == lane + FINE * block
    repeat = s % LANES == lane % FINE + FINE * block
    return [jnp.asarray(x.astype(jnp.bfloat16)) for x in (band, shift, repeat)]


def on_device(records, templates, fetch_list, cluster_slots, moveouts):
    n = fetch_list.shape[1]
    stations, comps, width = records.shape
    sets, nstat = cluster_slots.shape
    taps = templates.shape[-1]
    deep = -(-(taps + 2 * FINE - 1) // LANES) * LANES
    most = width - OUT - taps + 1
    wide = -(-(most // FINE + ROWS + PACK * (deep // LANES - 1)) // 8) * 8
    tall = -(-(most // FINE + ROWS + 1) // 8) * 8
    used = -(-(OUT + most) // LANES) * LANES
    tiles = sets * nstat // PACK
    rec_flat = jnp.transpose(records, (1, 0, 2)).reshape(comps * stations, width)
    kernels = jnp.transpose(templates, (0, 2, 1, 3))
    vmem = pl.BlockSpec(memory_space=pltpu.VMEM)
    far = pl.BlockSpec(memory_space=pltpu.HBM)
    one = pltpu.SemaphoreType.DMA
    stack, peak = pl.pallas_call(
        functools.partial(kernel, n, stations, sets, nstat, taps),
        out_shape=(
            pltpu.VMEM((sets, OUT), jnp.float32),
            pltpu.VMEM((1, OUT), jnp.float32),
        ),
        in_specs=[far] * 8,
        out_specs=(vmem, vmem),
        scratch_shapes=[
            pltpu.SMEM((fetch_list.shape[2], n), jnp.int32),
            pltpu.SMEM(cluster_slots.shape, jnp.int32),
            pltpu.SMEM(moveouts.shape, jnp.int32),
            pltpu.VMEM(rec_flat.shape, jnp.bfloat16),
            pltpu.VMEM(kernels.shape, jnp.bfloat16),
            pltpu.VMEM((n, 2, LANES), jnp.int32),
            pltpu.VMEM((n, 2, LANES), jnp.int32),
            pltpu.VMEM((n, 8, LANES), jnp.int32),
            pltpu.VMEM((n, 8, width), jnp.bfloat16),
            pltpu.VMEM((n, 8, width), jnp.bfloat16),
            pltpu.VMEM((3, deep // LANES, sets * nstat, LANES), jnp.float32),
            pltpu.VMEM((3, deep // LANES, sets * nstat, LANES), jnp.float32),
            pltpu.VMEM((3, sets * nstat, LANES), jnp.float32),
            pltpu.VMEM((3, tiles, deep, LANES), jnp.bfloat16),
            pltpu.VMEM((3, tiles, 8, LANES), jnp.float32),
            pltpu.VMEM((tiles, 8, LANES), jnp.int32),
            pltpu.VMEM((width, used), jnp.bfloat16),
            pltpu.VMEM((2 * LANES, PACK * LANES), jnp.bfloat16),
            pltpu.VMEM((2 * LANES, PACK * LANES), jnp.bfloat16),
            pltpu.VMEM((n * 6 * (wide + 1), LANES), jnp.float32),
            pltpu.VMEM((n * 6 * (tall + 1), LANES), jnp.float32),
            pltpu.SMEM((2, sets * nstat), jnp.int32),
            pltpu.VMEM((width // LANES, 96, LANES), jnp.float32),
            pltpu.VMEM((2, sets, LANES), jnp.float32),
            pltpu.VMEM((1, OUT), jnp.float32),
            pltpu.VMEM((n, 1, OUT), jnp.float32),
            pltpu.SemaphoreType.DMA((8,)),
            one, one, one, one, one, one,
        ],
        compiler_params=pltpu.CompilerParams(
            collective_id=0, has_side_effects=True, vmem_limit_bytes=60 << 20
        ),
        name="network_stack",
    )(jnp.transpose(fetch_list[0]), cluster_slots, moveouts, rec_flat, kernels,
      *masks(taps, width, used))
    anywhere = pl.BlockSpec(memory_space=pl.ANY)
    stack, peak = pl.pallas_call(
        hand_out,
        out_shape=(
            jax.ShapeDtypeStruct((sets, OUT), jnp.float32),
            jax.ShapeDtypeStruct((1, OUT), jnp.float32),
        ),
        in_specs=[vmem] * 2,
        out_specs=[anywhere] * 2,
        scratch_shapes=[pltpu.SemaphoreType.DMA((2,))],
        name="hand_out",
    )(*[pltpu.with_memory_space_constraint(x, pltpu.VMEM) for x in (stack, peak)])
    return stack, peak.reshape(OUT)


def solution(mesh):
    placed = (
        P(("groups", "tmpl"), None, None),
        P("tmpl", None, None, None),
        P("tmpl", None, None),
        P("tmpl", None),
        P("tmpl", None),
    )
    return jax.shard_map(
        on_device,
        mesh=mesh,
        in_specs=placed,
        out_specs=(P(("groups", "tmpl"), None), P("groups")),
        check_vma=False,
    )
```
